256 devices in a mesh: member: 4 (over x), vol: 64 (over z, y, core).
Axes of the slice: x: 4, y: 4, z: 8, core: 2. Of those that a mesh axis runs over, the one named last changes fastest.
Arguments:
- features: bfloat16 [32, 1024, 32, 128], P(None, 'vol'), may hold values from -6 to 6
- corner_z: int32 [64, 4], P('vol'), may hold values from 0 to 15, as said below
- corner_y: int32 [64, 4], P('vol'), may hold values from 0 to 24
- counts: int32 [64], P('vol'), may hold values from 0 to 4, as said below
- conv_w: bfloat16 [4, 32, 32, 3, 3, 3], P('member'), may hold values from -0.21875 to 0.21875
- norm_gain: float32 [4, 32], P('member'), may hold values from 0.1 to 1.9
- norm_shift: float32 [4, 32], P('member'), may hold values from -3 to 3
- seg_w: bfloat16 [4, 3, 32], P('member'), may hold values from -1 to 1
- seg_b: float32 [4, 3], P('member'), may hold values from -4 to 4
Outputs:
- probabilities: float32 [3, 1024, 32, 128], P(None, 'vol', 'member')
The draws below stay inside these ranges and needn't reach their ends.
Inputs may be any that keep to these rules, and one draw needn't show every extreme that they name: counts of slab s and slab s + 32 sum to exactly 4; slab 1 holds 4. `corner_z`: slot 0 of every slab has its corner at plane 16 - 1.
All inputs are finite; a program needn't handle non-finite values.
Results may differ from the reference program's by a relative error of at most 0.00059.
Values may be sent and summed in bfloat16 or wider, within the bound.
A program may use at most 128 MiB of HBM per device.

```python
import jax
import jax.numpy as jnp
from jax import lax

C = 32
K = 3
SZ = 16
SY = 32
X = 128
PZ = 4
PY = 8
MAXP = 4
PER_DEV = 2
SLABS = 64
MEMBERS = 4
Z = 1024


def draw_counts(key, part):
    half_count = SLABS // 2
    lowest = 2 * PER_DEV - MAXP
    first_half = jax.random.randint(key, (half_count,), lowest + 1, MAXP)
    first_half = first_half.at[1].set(MAXP)
    second_half = 2 * PER_DEV - first_half
    return jnp.concatenate([first_half, second_half]).astype(jnp.int32)


def draw_corner_z(key, part):
    corners = jax.random.randint(key, (SLABS, MAXP), 0, SZ)
    corners = corners.at[:, 0].set(SZ - 1)
    return corners.astype(jnp.int32)


def plant(drawn, key, smallest, high):
    shape = drawn.shape
    index_at = [jax.random.randint(jax.random.fold_in(key, axis), (), 0, shape[axis]) for axis in range(len(shape))]
    drawn = drawn.at[tuple(index_at)].set(smallest)
    longest = shape.index(max(shape))
    index_at[longest] = (index_at[longest] + 1) % shape[longest]
    return drawn.at[tuple(index_at)].set(high)


def shard_levels(key, shape, cuts, low, top_value):
    def one(dim, parts):
        draws = jax.random.uniform(jax.random.fold_in(jax.random.fold_in(key, 6), dim), (parts,), jnp.float32, low / len(cuts), top_value / len(cuts))
        return jnp.repeat(jnp.exp(draws), shape[dim] // parts).reshape((-1,) + (1,) * (len(shape) - dim - 1))

    factor_of = one(*cuts[0])
    for cut in cuts[1:]:
        factor_of = factor_of * one(*cut)
    return factor_of


def centred(key, extent, scale, bound, cuts=(), kind=jnp.bfloat16):
    result = scale * jax.random.normal(key, extent, jnp.float32)
    if cuts:
        result = result * shard_levels(key, extent, cuts, -0.22, 0.18)
    return jnp.clip(result, -bound, bound).astype(kind)


def setup_inputs(seed: int = 0) -> dict:
    keys = jax.random.split(jax.random.key(seed), 10)
    features = centred(keys[0], (C, Z, SY, X), 1.0, 6.0, ((1, 64),))
    corner_z = draw_corner_z(jax.random.fold_in(keys[9], 71), 0)
    corner_y = plant(jax.random.randint(keys[2], (SLABS, MAXP), 0, SY - PY + 1), jax.random.fold_in(keys[2], 1), 0, SY - PY).astype(jnp.int32)
    counts = draw_counts(jax.random.fold_in(keys[9], 71), 0)
    conv_w = centred(keys[4], (MEMBERS, C, C, 3, 3, 3), (27 * C) ** -0.5, 0.21875, ((0, 4),))
    norm_gain = jnp.clip(1.0 + 0.18 * jax.random.normal(keys[5], (MEMBERS, C), jnp.float32), 0.1, 1.9)
    norm_shift = centred(keys[6], (MEMBERS, C), 0.5, 3.0, ((0, 4),), jnp.float32)
    seg_w = centred(keys[7], (MEMBERS, K, C), C ** -0.5, 1.0, ((0, 4),))
    seg_b = centred(keys[8], (MEMBERS, K), 1.0, 4.0, ((0, 4),), jnp.float32)
    return dict(features=features, corner_z=corner_z, corner_y=corner_y, counts=counts, conv_w=conv_w, norm_gain=norm_gain, norm_shift=norm_shift, seg_w=seg_w, seg_b=seg_b)


def axis_weights(length):
    position = jnp.arange(length, dtype=jnp.float32)
    center = (length - 1) / 2.0
    sigma = length / 4.0
    return jnp.exp(-(position - center) ** 2 / (2.0 * sigma * sigma))

def gauss_table():
    return axis_weights(PZ)[:, None, None] * axis_weights(PY)[None, :, None] * axis_weights(X)[None, None, :]

def flip_fixed(volume_part, mirror):
    if mirror & 1:
        volume_part = jnp.flip(volume_part, -1)
    if mirror & 2:
        volume_part = jnp.flip(volume_part, -2)
    if mirror & 4:
        volume_part = jnp.flip(volume_part, -3)
    return volume_part

def network(patches, kernel, gain, offset, head, head_bias, mirror):
    flipped = flip_fixed(patches, mirror).astype(jnp.float32)
    hidden = lax.conv_general_dilated(flipped, kernel.astype(jnp.float32), (1, 1, 1), 'SAME', dimension_numbers=('NCDHW', 'OIDHW', 'NCDHW'), precision=lax.Precision.HIGHEST, preferred_element_type=jnp.float32)
    average = lax.optimization_barrier(jnp.mean(hidden, axis=(2, 3, 4), keepdims=True))
    variance = lax.optimization_barrier(jnp.mean((hidden - average) ** 2, axis=(2, 3, 4), keepdims=True))
    normed = (hidden - average) * lax.rsqrt(variance + 1e-05) * gain[None, :, None, None, None] + offset[None, :, None, None, None]
    normed = jnp.where(normed > 0, normed, 0.01 * normed)
    activation = normed.astype(jnp.bfloat16).astype(jnp.float32)
    logit = jnp.einsum('kc,ncdhw->nkdhw', head.astype(jnp.float32), activation, precision=lax.Precision.HIGHEST) + head_bias[None, :, None, None, None]
    return flip_fixed(logit, mirror)

def reference(features, corner_z, corner_y, counts, conv_w, norm_gain, norm_shift, seg_w, seg_b):
    extended = jnp.concatenate([features, jnp.zeros((C, PZ, SY, X), features.dtype)], axis=1)
    gaussian = gauss_table()
    totals = jnp.zeros((K + 1, SZ * SLABS + PZ, SY, X), jnp.float32)

    def per_slab(totals, slab_index):
        starts_z = corner_z[slab_index].astype(jnp.int32) + slab_index * SZ
        starts_y = corner_y[slab_index].astype(jnp.int32)

        def cut_patch(start_z, start_y):
            return lax.dynamic_slice(extended, (jnp.int32(0), start_z, start_y, jnp.int32(0)), (C, PZ, PY, X))
        patches = jax.vmap(cut_patch)(starts_z, starts_y)
        summed = jnp.zeros((MAXP, K, PZ, PY, X), jnp.float32)
        for member in range(MEMBERS):
            summed = summed + network(patches, conv_w[member], norm_gain[member], norm_shift[member], seg_w[member], seg_b[member], member % 8)
        alive = (jnp.arange(MAXP, dtype=jnp.int32) < counts[slab_index]).astype(jnp.float32)
        for slot_index in range(MAXP):
            placed = jnp.concatenate([summed[slot_index] * gaussian, (MEMBERS * gaussian)[None]], axis=0) * alive[slot_index]
            start = (jnp.int32(0), starts_z[slot_index], starts_y[slot_index], jnp.int32(0))
            totals = lax.dynamic_update_slice(totals, lax.dynamic_slice(totals, start, placed.shape) + placed, start)
        return (totals, None)
    totals, unused = lax.scan(per_slab, totals, jnp.arange(SLABS, dtype=jnp.int32))
    window = totals[:, :SZ * SLABS]
    average = window[:K] / jnp.maximum(window[K], 0.1)
    exponent = jnp.exp(average)
    return exponent / lax.optimization_barrier(jnp.sum(exponent, axis=0, keepdims=True))
```

```python
import functools

import jax
import jax.numpy as jnp
import numpy as np
from jax import lax
from jax.experimental import pallas as pl
from jax.experimental.pallas import tpu as pltpu
from jax.sharding import PartitionSpec as P

MESH = pl.DeviceIdType.MESH
C = 32
K = 3
PZ = 4
PY = 8
X = 128
MAXP = 4
M = 4
f32 = jnp.float32
bf16 = jnp.bfloat16


def bell(length):
    position = np.arange(length, dtype=np.float64)
    center = (length - 1) / 2.0
    sigma = length / 4.0
    return [float(v) for v in np.exp(-((position - center) ** 2) / (2.0 * sigma * sigma))]


def bell_x(shape):
    position = lax.broadcasted_iota(jnp.int32, shape, len(shape) - 1).astype(f32)
    center = (X - 1) / 2.0
    sigma = X / 4.0
    return jnp.exp(-((position - center) ** 2) / (2.0 * sigma * sigma))


def picked(values, index):
    out = jnp.full(index.shape, values[0], f32)
    for i in range(1, len(values)):
        out = jnp.where(index == i, f32(values[i]), out)
    return out


def kernel(
    depth, slabs,
    feat, cz_ref, cy_ref, cnt_ref, w_ref, gain_ref, shift_ref, segw_ref, segb_ref,
    out_ref,
    featv, staged, own, ints, ints_in, sendp, recvp, wall, prm, wa, wb, w9, seg, im, im9, hid,
    sums, tsend, tin, tback, pad_in, pad_own, gpad, inv,
    feat_sem, int_s, int_r, pl_s, pl_r, w_s, w_r, p_s, p_r, a_s, a_r, b_s, b_r, c_s, c_r,
):
    m = lax.axis_index("member")
    v = lax.axis_index("vol")
    nxt = lax.rem(v + 1, slabs)
    prv = lax.rem(v + slabs - 1, slabs)
    mates = [lax.rem(m + d, M) for d in range(1, M)]
    froms = [lax.rem(m + M - d, M) for d in range(1, M)]
    rows = featv.shape[2]

    feat_copy = pltpu.make_async_copy(feat, featv, feat_sem)
    feat_copy.start()

    barrier = pltpu.get_barrier_semaphore()
    for target in [(m, nxt), (m, prv)] + [(mate, v) for mate in mates]:
        pl.semaphore_signal(barrier, inc=1, device_id=target, device_id_type=MESH)

    lane = lax.broadcasted_iota(jnp.int32, (8, X), 1)
    row = jnp.where(lane == 8, cnt_ref[0], 0)
    for k in range(MAXP):
        row = jnp.where(lane == k, cz_ref[0, k], row)
        row = jnp.where(lane == 4 + k, cy_ref[0, k], row)
    ints[...] = row

    for kz in range(3):
        for ky in range(3):
            for kx in range(3):
                from_y = jnp.where((m // 2) % 2 == 1, 2 - ky, ky)
                from_x = jnp.where(m % 2 == 1, 2 - kx, kx)
                tap = w_ref[kz, from_y, from_x]
                t = ky * 3 + kx
                at = kz * 256 + t * C if t < 8 else 768 + kz * C
                wall[m, :, at:at + C] = tap
    prm[m] = jnp.zeros((8, X), f32)
    prm[m, 0:1, 0:C] = gain_ref[...]
    prm[m, 1:2, 0:C] = shift_ref[...]
    prm[m, 2:5, 0:C] = segw_ref[0].astype(f32)
    prm[m, 5:6, 0:K] = segb_ref[...]

    pl.semaphore_wait(barrier, 2 + len(mates))

    int_copy = pltpu.make_async_remote_copy(
        src_ref=ints, dst_ref=ints_in, send_sem=int_s, recv_sem=int_r,
        device_id=(m, nxt), device_id_type=MESH)
    int_copy.start()

    def shared(buf, send, recv, d):
        return pltpu.make_async_remote_copy(
            src_ref=buf.at[m], dst_ref=buf.at[m], send_sem=send.at[d], recv_sem=recv.at[d],
            device_id=(mates[d], v), device_id_type=MESH)

    def arrives(buf, send, recv, d):
        return pltpu.make_async_remote_copy(
            src_ref=buf.at[froms[d]], dst_ref=buf.at[froms[d]], send_sem=send.at[d], recv_sem=recv.at[d],
            device_id=(mates[d], v), device_id_type=MESH)

    for d in range(M - 1):
        shared(wall, w_s, w_r, d).start()
        shared(prm, p_s, p_r, d).start()

    def chosen(ref_row):
        value = ref_row(0)
        for k in range(1, MAXP):
            value = jnp.where(m == k, ref_row(k), value)
        return value

    my_z = chosen(lambda k: cz_ref[0, k])
    my_y = chosen(lambda k: cy_ref[0, k])
    feat_copy.wait()

    def plane_copy(j):
        return pltpu.make_async_remote_copy(
            src_ref=sendp.at[j], dst_ref=recvp.at[j], send_sem=pl_s.at[j], recv_sem=pl_r.at[j],
            device_id=(m, nxt), device_id_type=MESH)

    for j in range(PZ):
        z = jnp.minimum(my_z + j, depth - 1)

        def stage(c, carry, z=z):
            staged[pl.ds(c * rows, rows), :] = featv[c, z].astype(f32)
            return carry

        lax.fori_loop(0, C, stage, 0, unroll=8)

        def pick(y, carry, j=j):
            sendp[j, y] = staged[pl.ds(my_y + y, C, stride=rows), :].astype(bf16)
            return carry

        lax.fori_loop(0, PY, pick, 0, unroll=4)
        plane_copy(j).start()

    inside = (v > 0).astype(f32)
    for j in range(PZ - 1):
        def stage(c, carry, j=j):
            own[pl.ds(j * C * rows + c * rows, rows), :] = featv[c, j].astype(f32) * inside
            return carry

        lax.fori_loop(0, C, stage, 0, unroll=8)

    for j in range(PZ):
        for kx in range(3):
            im[j * 256 + kx * C:j * 256 + (kx + 1) * C, X:2 * X] = jnp.zeros((C, X), bf16)
        for kx in range(2):
            t = 6 + kx
            im[j * 256 + t * C:j * 256 + (t + 1) * C, 8 * X:9 * X] = jnp.zeros((C, X), bf16)
        im9[j * C:(j + 1) * C, 8 * X:9 * X] = jnp.zeros((C, X), bf16)

    int_copy.wait_recv()
    got = ints_in[...]
    prev_z = [jnp.sum(jnp.where(lane[0:1] == k, got[0:1], 0)) for k in range(MAXP)]
    prev_y = [jnp.sum(jnp.where(lane[0:1] == 4 + k, got[0:1], 0)) for k in range(MAXP)]
    prev_count = jnp.sum(jnp.where(lane[0:1] == 8, got[0:1], 0))
    at_z = chosen(lambda k: prev_z[k])
    at_y = chosen(lambda k: prev_y[k])

    gz, gy = bell(PZ), bell(PY)
    gyx = picked(gy, lax.broadcasted_iota(jnp.int32, (PY, X), 0)) * bell_x((PY, X))
    nothing = jnp.zeros((PY, X), f32)
    for j in range(PZ + 2):
        gpad[j, 0:8] = nothing
        gpad[j, 16:24] = nothing
        gpad[j, 8:16] = nothing if j in (0, PZ + 1) else gyx * (gz[j - 1] * M)
    for pad in (pad_in, pad_own):
        for s in range(MAXP):
            for j in range(PZ + 2):
                for k in range(K - 1):
                    pad[s, j, k, 0:8] = nothing
                    pad[s, j, k, 16:24] = nothing
                    if j in (0, PZ + 1):
                        pad[s, j, k, 8:16] = nothing

    first = m * PY
    own_off = [8 + jnp.clip(first - cy_ref[0, k], -8, 8) for k in range(MAXP)]
    in_off = [8 + jnp.clip(first - prev_y[k], -8, 8) for k in range(MAXP)]
    own_live = [(k < cnt_ref[0]).astype(f32) for k in range(MAXP)]
    in_live = [((k < prev_count) & (v > 0)).astype(f32) for k in range(MAXP)]

    def which(z):
        return 1 + jnp.clip(z, -1, PZ)

    def weigh(z, carry):
        total = jnp.zeros((PY, X), f32)
        for k in range(MAXP):
            total = total + gpad[which(z - cz_ref[0, k]), pl.ds(own_off[k], 8), :] * own_live[k]
            total = total + gpad[which(z + depth - prev_z[k]), pl.ds(in_off[k], 8), :] * in_live[k]
        inv[z] = 1.0 / jnp.maximum(total, 0.1)
        return carry

    lax.fori_loop(0, depth, weigh, 0)

    for d in range(M - 1):
        arrives(wall, w_s, w_r, d).wait_recv()
        arrives(prm, p_s, p_r, d).wait_recv()
    wa[...] = jnp.zeros(wa.shape, bf16)
    wb[...] = jnp.zeros(wb.shape, bf16)
    w9[...] = jnp.zeros(w9.shape, bf16)
    for q in range(M):
        r = q * C
        full = wall[q, :, 0:768]
        wa[r:r + C, 0:512] = full[:, 256:768]
        wa[128 + r:128 + r + C, :] = full
        wb[r:r + C, :] = full
        wb[128 + r:128 + r + C, 256:768] = full[:, 0:512]
        for o in range(PZ):
            for kz in range(3):
                j = o + kz - 1
                if 0 <= j < PZ:
                    w9[o * 128 + r:o * 128 + r + C, j * C:(j + 1) * C] = wall[q, :, 768 + kz * C:768 + (kz + 1) * C]

    def column(values):
        eye = lax.broadcasted_iota(jnp.int32, (C, C), 0) == lax.broadcasted_iota(jnp.int32, (C, C), 1)
        return jnp.sum(jnp.where(eye, jnp.broadcast_to(values, (C, C)), 0.0), axis=1, keepdims=True)

    gain = jnp.concatenate([column(prm[q, 0:1, 0:C]) for q in range(M)], axis=0)
    shift = jnp.concatenate([column(prm[q, 1:2, 0:C]) for q in range(M)], axis=0)
    seg[...] = jnp.zeros(seg.shape, f32)
    for q in range(M):
        for o in range(2):
            at = o * 128 + q * C
            for k in range(K - 1):
                seg[k * 2 + o:k * 2 + o + 1, at:at + C] = prm[q, 2 + k:3 + k, 0:C]
                seg[8 + k * 2 + o:8 + k * 2 + o + 1, at:at + C] = prm[q, 4:5, 0:C]
    head = seg[...].astype(bf16)
    offsets = prm[0, 5:6, :] + prm[1, 5:6, :] + prm[2, 5:6, :] + prm[3, 5:6, :]
    offset = [jnp.sum(jnp.where(lane[0:1] == k, offsets, 0.0)) for k in range(K)]
    sub = lax.broadcasted_iota(jnp.int32, (8, 1), 0)
    bias = jnp.where(sub < 2, offset[0] - offset[2], offset[1] - offset[2])

    lane_row = lax.broadcasted_iota(jnp.int32, (C, X), 1)
    for j in range(PZ):
        plane_copy(j).wait_recv()
        beyond = at_z + j - depth
        start = jnp.clip(beyond, 0, PZ - 2) * (C * rows) + at_y

        def expand(y, carry, j=j, beyond=beyond, start=start):
            value = recvp[j, y].astype(f32)
            if j > 0:
                value = jnp.where(beyond >= 0, own[pl.ds(start + y, C, stride=rows), :], value)
            left = jnp.where(lane_row == 0, 0.0, pltpu.roll(value, 1, 1)).astype(bf16)
            right = jnp.where(lane_row == X - 1, 0.0, pltpu.roll(value, X - 1, 1)).astype(bf16)
            middle = value.astype(bf16)
            for ky in range(3):
                at = pl.ds(pl.multiple_of((y - ky + 2) * X, X), X)
                for kx, part in enumerate((left, middle, right)):
                    t = ky * 3 + kx
                    if t < 8:
                        im[j * 256 + t * C:j * 256 + (t + 1) * C, at] = part
                    else:
                        im9[j * C:(j + 1) * C, at] = part
            return carry

        lax.fori_loop(0, PY, expand, 0, unroll=2)

    sums[...] = jnp.zeros(sums.shape, f32)
    for p, taps in enumerate((wa, wb)):
        def conv(n, carry, p=p, taps=taps):
            at = pl.ds(pl.multiple_of(X + n * 256, X), 256)
            got = jnp.dot(taps[...], im[p * 256:p * 256 + 768, at], preferred_element_type=f32)
            got = got + jnp.dot(w9[p * 256:(p + 1) * 256, :], im9[:, at], preferred_element_type=f32)
            hid[p, :, pl.ds(pl.multiple_of(n * 256, 256), 256)] = got
            pair = got[:128] + got[128:]
            sums[...] += pair[:, :X] + pair[:, X:]
            return carry

        lax.fori_loop(0, 4, conv, 0)

    voxels = PZ * PY * X
    mean = jnp.sum(sums[...], axis=1, keepdims=True) / voxels
    sums[...] = jnp.zeros(sums.shape, f32)
    for p in range(2):
        def spread(n, carry, p=p):
            got = hid[p, :, pl.ds(pl.multiple_of(n * 256, 256), 256)]
            low = got[:128] - mean
            high = got[128:] - mean
            pair = low * low + high * high
            sums[...] += pair[:, :X] + pair[:, X:]
            return carry

        lax.fori_loop(0, 4, spread, 0)
    variance = jnp.sum(sums[...], axis=1, keepdims=True) / voxels
    scale = lax.rsqrt(variance + 1e-05) * gain

    alive = m < prev_count
    gx = bell_x((8, X))
    for p in range(2):
        gzp = jnp.where(sub % 2 == 0, f32(gz[2 * p]), f32(gz[2 * p + 1]))

        def classify(n, carry, p=p, gzp=gzp):
            parts = []
            for o in range(2):
                got = hid[p, o * 128:(o + 1) * 128, pl.ds(pl.multiple_of(n * 256, 256), 256)]
                normed = (got - mean) * scale + shift
                parts.append(jnp.maximum(normed, 0.01 * normed).astype(bf16))
            act = jnp.concatenate(parts, axis=0)
            both = jnp.dot(head, act, preferred_element_type=f32)
            logit = both[0:8] - both[8:16] + bias
            for h in range(2):
                y = n * 2 + h
                gyv = f32(gy[0])
                for i in range(1, PY):
                    gyv = jnp.where(y == i, f32(gy[i]), gyv)
                value = logit[:, h * X:(h + 1) * X] * (gx * gzp * gyv)
                value = jnp.where(alive, value, 0.0)
                tsend[p, pl.ds(y, 8, stride=8), :] = value
            return carry

        lax.fori_loop(0, 4, classify, 0)

    back = pltpu.make_async_remote_copy(
        src_ref=tsend.at[:, pl.ds(0, 32)], dst_ref=tback.at[m], send_sem=b_s, recv_sem=b_r,
        device_id=(m, prv), device_id_type=MESH)
    back.start()

    def across(d):
        return pltpu.make_async_remote_copy(
            src_ref=tsend.at[:, pl.ds(0, 32)], dst_ref=tin.at[m], send_sem=a_s.at[d], recv_sem=a_r.at[d],
            device_id=(mates[d], v), device_id_type=MESH)

    for d in range(M - 1):
        across(d).start()
    back.wait_recv()
    for d in range(M - 1):
        shared(tback, c_s, c_r, d).start()
    tin[m] = tsend[:, 0:32]

    def spread_out(buf, pad, s):
        for p in range(2):
            for k in range(K - 1):
                for o in range(2):
                    r = (k * 2 + o) * 8
                    pad[s, 1 + 2 * p + o, k, 8:16] = buf[s, p, r:r + 8]

    for d in range(M - 1):
        arrives(tin, a_s, a_r, d).wait_recv()
    for s in range(MAXP):
        spread_out(tin, pad_in, s)
    for d in range(M - 1):
        arrives(tback, c_s, c_r, d).wait_recv()
    for s in range(MAXP):
        spread_out(tback, pad_own, s)

    def finish(z, spill):
        diff = []
        for k in range(K - 1):
            total = jnp.zeros((PY, X), f32)
            for s in range(MAXP):
                total = total + pad_own[s, which(z - cz_ref[0, s]), k, pl.ds(own_off[s], 8), :]
                if spill:
                    total = total + pad_in[s, which(z + depth - prev_z[s]), k, pl.ds(in_off[s], 8), :] * inside
            diff.append(total * inv[z])
        top = jnp.maximum(jnp.maximum(diff[0], diff[1]), 0.0)
        powers = [jnp.exp(diff[0] - top), jnp.exp(diff[1] - top), jnp.exp(-top)]
        whole = 1.0 / (powers[0] + powers[1] + powers[2])
        for k in range(K):
            out_ref[k, z] = powers[k] * whole

    for z in range(PZ - 1):
        finish(z, True)

    def rest(z, carry):
        finish(z, False)
        return carry

    lax.fori_loop(PZ - 1, depth, rest, 0)

    int_copy.wait_send()
    for j in range(PZ):
        plane_copy(j).wait_send()
    back.wait_send()
    for d in range(M - 1):
        shared(wall, w_s, w_r, d).wait_send()
        shared(prm, p_s, p_r, d).wait_send()
        across(d).wait_send()
        shared(tback, c_s, c_r, d).wait_send()


def per_device(slabs, features, corner_z, corner_y, counts, conv_w, norm_gain, norm_shift, seg_w, seg_b):
    channels, depth, rows, width = features.shape
    taps = conv_w[0].transpose(2, 3, 4, 0, 1)
    smem = pl.BlockSpec(memory_space=pltpu.SMEM)
    vmem = pl.BlockSpec(memory_space=pltpu.VMEM)
    dma = pltpu.SemaphoreType.DMA
    return pl.pallas_call(
        functools.partial(kernel, depth, slabs),
        name="ensemble_patches",
        out_shape=jax.ShapeDtypeStruct((K, depth, rows // M, width), f32),
        in_specs=[pl.BlockSpec(memory_space=pl.ANY), smem, smem, smem] + [vmem] * 5,
        out_specs=vmem,
        scratch_shapes=[
            pltpu.VMEM((channels, depth, rows, width), bf16),
            pltpu.VMEM((C * rows, X), f32),
            pltpu.VMEM(((PZ - 1) * C * rows, X), f32),
            pltpu.VMEM((8, X), jnp.int32),
            pltpu.VMEM((8, X), jnp.int32),
            pltpu.VMEM((PZ, PY, C, X), bf16),
            pltpu.VMEM((PZ, PY, C, X), bf16),
            pltpu.VMEM((M, C, 896), bf16),
            pltpu.VMEM((M, 8, X), f32),
            pltpu.VMEM((256, 768), bf16),
            pltpu.VMEM((256, 768), bf16),
            pltpu.VMEM((512, 128), bf16),
            pltpu.VMEM((16, 256), f32),
            pltpu.VMEM((PZ * 256, 10 * X), bf16),
            pltpu.VMEM((PZ * C, 10 * X), bf16),
            pltpu.VMEM((2, 256, PY * X), f32),
            pltpu.VMEM((128, X), f32),
            pltpu.VMEM((2, 64, X), f32),
            pltpu.VMEM((M, 2, 32, X), f32),
            pltpu.VMEM((M, 2, 32, X), f32),
            pltpu.VMEM((MAXP, PZ + 2, K - 1, 24, X), f32),
            pltpu.VMEM((MAXP, PZ + 2, K - 1, 24, X), f32),
            pltpu.VMEM((PZ + 2, 24, X), f32),
            pltpu.VMEM((depth, PY, X), f32),
            dma, dma, dma, dma((PZ,)), dma((PZ,)), dma((3,)), dma((3,)), dma((3,)), dma((3,)),
            dma((3,)), dma((3,)), dma, dma, dma((3,)), dma((3,)),
        ],
        compiler_params=pltpu.CompilerParams(
            collective_id=0, has_side_effects=True, vmem_limit_bytes=40 * 1024 * 1024),
    )(features, corner_z, corner_y, counts, taps, norm_gain, norm_shift, seg_w, seg_b)


def solution(mesh):
    placed = (
        P(None, "vol", None, None),
        P("vol", None),
        P("vol", None),
        P("vol"),
        P("member", None, None, None, None, None),
        P("member", None),
        P("member", None),
        P("member", None, None),
        P("member", None),
    )
    return jax.shard_map(
        functools.partial(per_device, mesh.shape["vol"]),
        mesh=mesh,
        in_specs=placed,
        out_specs=P(None, "vol", "member", None),
        check_vma=False,
    )
```

```python
import functools

import jax
import jax.numpy as jnp
import numpy as np
from jax import lax
from jax.experimental import pallas as pl
from jax.experimental.pallas import tpu as pltpu
from jax.sharding import PartitionSpec as P

MESH = pl.DeviceIdType.MESH
C = 32
K = 3
PZ = 4
PY = 8
X = 128
MAXP = 4
M = 4
f32 = jnp.float32
bf16 = jnp.bfloat16


def bell(length):
    position = np.arange(length, dtype=np.float64)
    center = (length - 1) / 2.0
    sigma = length / 4.0
    return [float(v) for v in np.exp(-((position - center) ** 2) / (2.0 * sigma * sigma))]


def bell_x(shape):
    position = lax.broadcasted_iota(jnp.int32, shape, len(shape) - 1).astype(f32)
    center = (X - 1) / 2.0
    sigma = X / 4.0
    return jnp.exp(-((position - center) ** 2) / (2.0 * sigma * sigma))


def picked(values, index):
    out = jnp.full(index.shape, values[0], f32)
    for i in range(1, len(values)):
        out = jnp.where(index == i, f32(values[i]), out)
    return out


def kernel(
    depth, slabs,
    feat, cz_hbm, cy_hbm, cnt_hbm, w_hbm, gain_hbm, shift_hbm, segw_hbm, segb_hbm,
    out_ref,
    cz_ref, cy_ref, cnt_ref, w_ref, gain_ref, shift_ref, segw_ref, segb_ref, featv, staged, own, ints, ints_in, sendp, recvp, wall, prm, wa, wb, w9, seg, im, im9, hid,
    sums, tsend, tin, tback, pad_in, pad_own, gpad, inv,
    small_sem, feat_sem, int_s, int_r, pl_s, pl_r, w_s, w_r, p_s, p_r, a_s, a_r, b_s, b_r, c_s, c_r,
):
    m = lax.axis_index("member")
    v = lax.axis_index("vol")
    nxt = lax.rem(v + 1, slabs)
    prv = lax.rem(v + slabs - 1, slabs)
    mates = [lax.rem(m + d, M) for d in range(1, M)]
    froms = [lax.rem(m + M - d, M) for d in range(1, M)]
    rows = featv.shape[2]

    small = [
        pltpu.make_async_copy(src, dst, small_sem.at[i])
        for i, (src, dst) in enumerate((
            (cz_hbm, cz_ref), (cy_hbm, cy_ref), (cnt_hbm, cnt_ref), (w_hbm, w_ref), (gain_hbm, gain_ref),
            (shift_hbm, shift_ref), (segw_hbm, segw_ref), (segb_hbm, segb_ref)))
    ]
    for copy in small:
        copy.start()
    feat_copy = pltpu.make_async_copy(feat, featv, feat_sem)
    feat_copy.start()

    barrier = pltpu.get_barrier_semaphore()
    for target in [(m, nxt), (m, prv)] + [(mate, v) for mate in mates]:
        pl.semaphore_signal(barrier, inc=1, device_id=target, device_id_type=MESH)

    for copy in small:
        copy.wait()

    lane = lax.broadcasted_iota(jnp.int32, (8, X), 1)
    row = jnp.where(lane == 8, cnt_ref[0], 0)
    for k in range(MAXP):
        row = jnp.where(lane == k, cz_ref[0, k], row)
        row = jnp.where(lane == 4 + k, cy_ref[0, k], row)
    ints[...] = row

    for kz in range(3):
        for ky in range(3):
            for kx in range(3):
                from_y = jnp.where((m // 2) % 2 == 1, 2 - ky, ky)
                from_x = jnp.where(m % 2 == 1, 2 - kx, kx)
                tap = w_ref[kz, from_y, from_x]
                t = ky * 3 + kx
                at = kz * 256 + t * C if t < 8 else 768 + kz * C
                wall[m, :, at:at + C] = tap
    prm[m] = jnp.zeros((8, X), f32)
    prm[m, 0:1, 0:C] = gain_ref[...]
    prm[m, 1:2, 0:C] = shift_ref[...]
    prm[m, 2:5, 0:C] = segw_ref[0].astype(f32)
    prm[m, 5:6, 0:K] = segb_ref[...]

    pl.semaphore_wait(barrier, 2 + len(mates))

    int_copy = pltpu.make_async_remote_copy(
        src_ref=ints, dst_ref=ints_in, send_sem=int_s, recv_sem=int_r,
        device_id=(m, nxt), device_id_type=MESH)
    int_copy.start()

    def shared(buf, send, recv, d):
        return pltpu.make_async_remote_copy(
            src_ref=buf.at[m], dst_ref=buf.at[m], send_sem=send.at[d], recv_sem=recv.at[d],
            device_id=(mates[d], v), device_id_type=MESH)

    def arrives(buf, send, recv, d):
        return pltpu.make_async_remote_copy(
            src_ref=buf.at[froms[d]], dst_ref=buf.at[froms[d]], send_sem=send.at[d], recv_sem=recv.at[d],
            device_id=(mates[d], v), device_id_type=MESH)

    for d in range(M - 1):
        shared(wall, w_s, w_r, d).start()
        shared(prm, p_s, p_r, d).start()

    def chosen(ref_row):
        value = ref_row(0)
        for k in range(1, MAXP):
            value = jnp.where(m == k, ref_row(k), value)
        return value

    my_z = chosen(lambda k: cz_ref[0, k])
    my_y = chosen(lambda k: cy_ref[0, k])
    feat_copy.wait()

    def plane_copy(j):
        return pltpu.make_async_remote_copy(
            src_ref=sendp.at[j], dst_ref=recvp.at[j], send_sem=pl_s.at[j], recv_sem=pl_r.at[j],
            device_id=(m, nxt), device_id_type=MESH)

    for j in range(PZ):
        z = jnp.minimum(my_z + j, depth - 1)

        def stage(c, carry, z=z):
            staged[pl.ds(c * rows, rows), :] = featv[c, z].astype(f32)
            return carry

        lax.fori_loop(0, C, stage, 0, unroll=8)

        def pick(y, carry, j=j):
            sendp[j, y] = staged[pl.ds(my_y + y, C, stride=rows), :].astype(bf16)
            return carry

        lax.fori_loop(0, PY, pick, 0, unroll=4)
        plane_copy(j).start()

    inside = (v > 0).astype(f32)
    for j in range(PZ - 1):
        def stage(c, carry, j=j):
            own[pl.ds(j * C * rows + c * rows, rows), :] = featv[c, j].astype(f32) * inside
            return carry

        lax.fori_loop(0, C, stage, 0, unroll=8)

    for j in range(PZ):
        for kx in range(3):
            im[j * 256 + kx * C:j * 256 + (kx + 1) * C, X:2 * X] = jnp.zeros((C, X), bf16)
        for kx in range(2):
            t = 6 + kx
            im[j * 256 + t * C:j * 256 + (t + 1) * C, 8 * X:9 * X] = jnp.zeros((C, X), bf16)
        im9[j * C:(j + 1) * C, 8 * X:9 * X] = jnp.zeros((C, X), bf16)

    int_copy.wait_recv()
    got = ints_in[...]
    prev_z = [jnp.sum(jnp.where(lane[0:1] == k, got[0:1], 0)) for k in range(MAXP)]
    prev_y = [jnp.sum(jnp.where(lane[0:1] == 4 + k, got[0:1], 0)) for k in range(MAXP)]
    prev_count = jnp.sum(jnp.where(lane[0:1] == 8, got[0:1], 0))
    at_z = chosen(lambda k: prev_z[k])
    at_y = chosen(lambda k: prev_y[k])

    gz, gy = bell(PZ), bell(PY)
    gyx = picked(gy, lax.broadcasted_iota(jnp.int32, (PY, X), 0)) * bell_x((PY, X))
    nothing = jnp.zeros((PY, X), f32)
    for j in range(PZ + 2):
        gpad[j, 0:8] = nothing
        gpad[j, 16:24] = nothing
        gpad[j, 8:16] = nothing if j in (0, PZ + 1) else gyx * (gz[j - 1] * M)
    for pad in (pad_in, pad_own):
        for s in range(MAXP):
            for j in range(PZ + 2):
                for k in range(K - 1):
                    pad[s, j, k, 0:8] = nothing
                    pad[s, j, k, 16:24] = nothing
                    if j in (0, PZ + 1):
                        pad[s, j, k, 8:16] = nothing

    first = m * PY
    own_off = [8 + jnp.clip(first - cy_ref[0, k], -8, 8) for k in range(MAXP)]
    in_off = [8 + jnp.clip(first - prev_y[k], -8, 8) for k in range(MAXP)]
    own_live = [(k < cnt_ref[0]).astype(f32) for k in range(MAXP)]
    in_live = [((k < prev_count) & (v > 0)).astype(f32) for k in range(MAXP)]

    def which(z):
        return 1 + jnp.clip(z, -1, PZ)

    def weigh(z, carry):
        total = jnp.zeros((PY, X), f32)
        for k in range(MAXP):
            total = total + gpad[which(z - cz_ref[0, k]), pl.ds(own_off[k], 8), :] * own_live[k]
            total = total + gpad[which(z + depth - prev_z[k]), pl.ds(in_off[k], 8), :] * in_live[k]
        inv[z] = 1.0 / jnp.maximum(total, 0.1)
        return carry

    lax.fori_loop(0, depth, weigh, 0)

    for d in range(M - 1):
        arrives(wall, w_s, w_r, d).wait_recv()
        arrives(prm, p_s, p_r, d).wait_recv()
    wa[...] = jnp.zeros(wa.shape, bf16)
    wb[...] = jnp.zeros(wb.shape, bf16)
    w9[...] = jnp.zeros(w9.shape, bf16)
    for q in range(M):
        r = q * C
        full = wall[q, :, 0:768]
        wa[r:r + C, 0:512] = full[:, 256:768]
        wa[128 + r:128 + r + C, :] = full
        wb[r:r + C, :] = full
        wb[128 + r:128 + r + C, 256:768] = full[:, 0:512]
        for o in range(PZ):
            for kz in range(3):
                j = o + kz - 1
                if 0 <= j < PZ:
                    w9[o * 128 + r:o * 128 + r + C, j * C:(j + 1) * C] = wall[q, :, 768 + kz * C:768 + (kz + 1) * C]

    def column(values):
        eye = lax.broadcasted_iota(jnp.int32, (C, C), 0) == lax.broadcasted_iota(jnp.int32, (C, C), 1)
        return jnp.sum(jnp.where(eye, jnp.broadcast_to(values, (C, C)), 0.0), axis=1, keepdims=True)

    gain = jnp.concatenate([column(prm[q, 0:1, 0:C]) for q in range(M)], axis=0)
    shift = jnp.concatenate([column(prm[q, 1:2, 0:C]) for q in range(M)], axis=0)
    seg[...] = jnp.zeros(seg.shape, f32)
    for q in range(M):
        for o in range(2):
            at = o * 128 + q * C
            for k in range(K - 1):
                seg[k * 2 + o:k * 2 + o + 1, at:at + C] = prm[q, 2 + k:3 + k, 0:C]
                seg[8 + k * 2 + o:8 + k * 2 + o + 1, at:at + C] = prm[q, 4:5, 0:C]
    head = seg[...].astype(bf16)
    offsets = prm[0, 5:6, :] + prm[1, 5:6, :] + prm[2, 5:6, :] + prm[3, 5:6, :]
    offset = [jnp.sum(jnp.where(lane[0:1] == k, offsets, 0.0)) for k in range(K)]
    sub = lax.broadcasted_iota(jnp.int32, (8, 1), 0)
    bias = jnp.where(sub < 2, offset[0] - offset[2], offset[1] - offset[2])

    lane_row = lax.broadcasted_iota(jnp.int32, (C, X), 1)
    for j in range(PZ):
        plane_copy(j).wait_recv()
        beyond = at_z + j - depth
        start = jnp.clip(beyond, 0, PZ - 2) * (C * rows) + at_y

        def expand(y, carry, j=j, beyond=beyond, start=start):
            value = recvp[j, y].astype(f32)
            if j > 0:
                value = jnp.where(beyond >= 0, own[pl.ds(start + y, C, stride=rows), :], value)
            left = jnp.where(lane_row == 0, 0.0, pltpu.roll(value, 1, 1)).astype(bf16)
            right = jnp.where(lane_row == X - 1, 0.0, pltpu.roll(value, X - 1, 1)).astype(bf16)
            middle = value.astype(bf16)
            for ky in range(3):
                at = pl.ds(pl.multiple_of((y - ky + 2) * X, X), X)
                for kx, part in enumerate((left, middle, right)):
                    t = ky * 3 + kx
                    if t < 8:
                        im[j * 256 + t * C:j * 256 + (t + 1) * C, at] = part
                    else:
                        im9[j * C:(j + 1) * C, at] = part
            return carry

        lax.fori_loop(0, PY, expand, 0, unroll=2)

    sums[...] = jnp.zeros(sums.shape, f32)
    for p, taps in enumerate((wa, wb)):
        def conv(n, carry, p=p, taps=taps):
            at = pl.ds(pl.multiple_of(X + n * 256, X), 256)
            got = jnp.dot(taps[...], im[p * 256:p * 256 + 768, at], preferred_element_type=f32)
            got = got + jnp.dot(w9[p * 256:(p + 1) * 256, :], im9[:, at], preferred_element_type=f32)
            hid[p, :, pl.ds(pl.multiple_of(n * 256, 256), 256)] = got
            pair = got[:128] + got[128:]
            sums[...] += pair[:, :X] + pair[:, X:]
            return carry

        lax.fori_loop(0, 4, conv, 0)

    voxels = PZ * PY * X
    mean = jnp.sum(sums[...], axis=1, keepdims=True) / voxels
    sums[...] = jnp.zeros(sums.shape, f32)
    for p in range(2):
        def spread(n, carry, p=p):
            got = hid[p, :, pl.ds(pl.multiple_of(n * 256, 256), 256)]
            low = got[:128] - mean
            high = got[128:] - mean
            pair = low * low + high * high
            sums[...] += pair[:, :X] + pair[:, X:]
            return carry

        lax.fori_loop(0, 4, spread, 0)
    variance = jnp.sum(sums[...], axis=1, keepdims=True) / voxels
    scale = lax.rsqrt(variance + 1e-05) * gain

    alive = m < prev_count
    gx = bell_x((8, X))
    for p in range(2):
        gzp = jnp.where(sub % 2 == 0, f32(gz[2 * p]), f32(gz[2 * p + 1]))

        def classify(n, carry, p=p, gzp=gzp):
            parts = []
            for o in range(2):
                got = hid[p, o * 128:(o + 1) * 128, pl.ds(pl.multiple_of(n * 256, 256), 256)]
                normed = (got - mean) * scale + shift
                parts.append(jnp.maximum(normed, 0.01 * normed).astype(bf16))
            act = jnp.concatenate(parts, axis=0)
            both = jnp.dot(head, act, preferred_element_type=f32)
            logit = both[0:8] - both[8:16] + bias
            for h in range(2):
                y = n * 2 + h
                gyv = f32(gy[0])
                for i in range(1, PY):
                    gyv = jnp.where(y == i, f32(gy[i]), gyv)
                value = logit[:, h * X:(h + 1) * X] * (gx * gzp * gyv)
                value = jnp.where(alive, value, 0.0)
                tsend[p, pl.ds(y, 8, stride=8), :] = value
            return carry

        lax.fori_loop(0, 4, classify, 0)

    back = pltpu.make_async_remote_copy(
        src_ref=tsend.at[:, pl.ds(0, 32)], dst_ref=tback.at[m], send_sem=b_s, recv_sem=b_r,
        device_id=(m, prv), device_id_type=MESH)
    back.start()

    def across(d):
        return pltpu.make_async_remote_copy(
            src_ref=tsend.at[:, pl.ds(0, 32)], dst_ref=tin.at[m], send_sem=a_s.at[d], recv_sem=a_r.at[d],
            device_id=(mates[d], v), device_id_type=MESH)

    for d in range(M - 1):
        across(d).start()
    back.wait_recv()
    for d in range(M - 1):
        shared(tback, c_s, c_r, d).start()
    tin[m] = tsend[:, 0:32]

    def spread_out(buf, pad, s):
        for p in range(2):
            for k in range(K - 1):
                for o in range(2):
                    r = (k * 2 + o) * 8
                    pad[s, 1 + 2 * p + o, k, 8:16] = buf[s, p, r:r + 8]

    for d in range(M - 1):
        arrives(tin, a_s, a_r, d).wait_recv()
    for s in range(MAXP):
        spread_out(tin, pad_in, s)
    for d in range(M - 1):
        arrives(tback, c_s, c_r, d).wait_recv()
    for s in range(MAXP):
        spread_out(tback, pad_own, s)

    def finish(z, spill):
        diff = []
        for k in range(K - 1):
            total = jnp.zeros((PY, X), f32)
            for s in range(MAXP):
                total = total + pad_own[s, which(z - cz_ref[0, s]), k, pl.ds(own_off[s], 8), :]
                if spill:
                    total = total + pad_in[s, which(z + depth - prev_z[s]), k, pl.ds(in_off[s], 8), :] * inside
            diff.append(total * inv[z])
        top = jnp.maximum(jnp.maximum(diff[0], diff[1]), 0.0)
        powers = [jnp.exp(diff[0] - top), jnp.exp(diff[1] - top), jnp.exp(-top)]
        whole = 1.0 / (powers[0] + powers[1] + powers[2])
        for k in range(K):
            out_ref[k, z] = powers[k] * whole

    for z in range(PZ - 1):
        finish(z, True)

    def rest(z, carry):
        finish(z, False)
        return carry

    lax.fori_loop(PZ - 1, depth, rest, 0)

    int_copy.wait_send()
    for j in range(PZ):
        plane_copy(j).wait_send()
    back.wait_send()
    for d in range(M - 1):
        shared(wall, w_s, w_r, d).wait_send()
        shared(prm, p_s, p_r, d).wait_send()
        across(d).wait_send()
        shared(tback, c_s, c_r, d).wait_send()


def per_device(slabs, features, corner_z, corner_y, counts, conv_w, norm_gain, norm_shift, seg_w, seg_b):
    channels, depth, rows, width = features.shape
    taps = conv_w[0].transpose(2, 3, 4, 0, 1)
    dma = pltpu.SemaphoreType.DMA
    return pl.pallas_call(
        functools.partial(kernel, depth, slabs),
        name="ensemble_patches",
        out_shape=jax.ShapeDtypeStruct((K, depth, rows // M, width), f32),
        in_specs=[pl.BlockSpec(memory_space=pltpu.HBM)] * 9,
        out_specs=pl.BlockSpec(memory_space=pltpu.VMEM),
        scratch_shapes=[
            pltpu.SMEM((1, MAXP), jnp.int32),
            pltpu.SMEM((1, MAXP), jnp.int32),
            pltpu.SMEM((1,), jnp.int32),
            pltpu.VMEM((3, 3, 3, C, C), bf16),
            pltpu.VMEM((1, C), f32),
            pltpu.VMEM((1, C), f32),
            pltpu.VMEM((1, K, C), bf16),
            pltpu.VMEM((1, K), f32),
            pltpu.VMEM((channels, depth, rows, width), bf16),
            pltpu.VMEM((C * rows, X), f32),
            pltpu.VMEM(((PZ - 1) * C * rows, X), f32),
            pltpu.VMEM((8, X), jnp.int32),
            pltpu.VMEM((8, X), jnp.int32),
            pltpu.VMEM((PZ, PY, C, X), bf16),
            pltpu.VMEM((PZ, PY, C, X), bf16),
            pltpu.VMEM((M, C, 896), bf16),
            pltpu.VMEM((M, 8, X), f32),
            pltpu.VMEM((256, 768), bf16),
            pltpu.VMEM((256, 768), bf16),
            pltpu.VMEM((512, 128), bf16),
            pltpu.VMEM((16, 256), f32),
            pltpu.VMEM((PZ * 256, 10 * X), bf16),
            pltpu.VMEM((PZ * C, 10 * X), bf16),
            pltpu.VMEM((2, 256, PY * X), f32),
            pltpu.VMEM((128, X), f32),
            pltpu.VMEM((2, 64, X), f32),
            pltpu.VMEM((M, 2, 32, X), f32),
            pltpu.VMEM((M, 2, 32, X), f32),
            pltpu.VMEM((MAXP, PZ + 2, K - 1, 24, X), f32),
            pltpu.VMEM((MAXP, PZ + 2, K - 1, 24, X), f32),
            pltpu.VMEM((PZ + 2, 24, X), f32),
            pltpu.VMEM((depth, PY, X), f32),
            dma((8,)), dma, dma, dma, dma((PZ,)), dma((PZ,)), dma((3,)), dma((3,)), dma((3,)), dma((3,)),
            dma((3,)), dma((3,)), dma, dma, dma((3,)), dma((3,)),
        ],
        compiler_params=pltpu.CompilerParams(
            collective_id=0, has_side_effects=True, vmem_limit_bytes=40 * 1024 * 1024),
    )(features, corner_z, corner_y, counts, taps, norm_gain, norm_shift, seg_w, seg_b)


def solution(mesh):
    placed = (
        P(None, "vol", None, None),
        P("vol", None),
        P("vol", None),
        P("vol"),
        P("member", None, None, None, None, None),
        P("member", None),
        P("member", None),
        P("member", None, None),
        P("member", None),
    )
    return jax.shard_map(
        functools.partial(per_device, mesh.shape["vol"]),
        mesh=mesh,
        in_specs=placed,
        out_specs=P(None, "vol", "member", None),
        check_vma=False,
    )
```

```python
import functools

import jax
import jax.numpy as jnp
import numpy as np
from jax import lax
from jax.experimental import pallas as pl
from jax.experimental.pallas import tpu as pltpu
from jax.sharding import PartitionSpec as P

MESH = pl.DeviceIdType.MESH
C = 32
K = 3
PZ = 4
PY = 8
X = 128
MAXP = 4
M = 4
f32 = jnp.float32
bf16 = jnp.bfloat16


def bell(length):
    position = np.arange(length, dtype=np.float64)
    center = (length - 1) / 2.0
    sigma = length / 4.0
    return [float(v) for v in np.exp(-((position - center) ** 2) / (2.0 * sigma * sigma))]


def bell_x(shape):
    position = lax.broadcasted_iota(jnp.int32, shape, len(shape) - 1).astype(f32)
    center = (X - 1) / 2.0
    sigma = X / 4.0
    return jnp.exp(-((position - center) ** 2) / (2.0 * sigma * sigma))


def picked(values, index):
    out = jnp.full(index.shape, values[0], f32)
    for i in range(1, len(values)):
        out = jnp.where(index == i, f32(values[i]), out)
    return out


def kernel(
    depth, slabs,
    feat, cz_hbm, cy_hbm, cnt_hbm, w_hbm, gain_hbm, shift_hbm, segw_hbm, segb_hbm,
    out_hbm,
    cz_ref, cy_ref, cnt_ref, w_ref, gain_ref, shift_ref, segw_ref, segb_ref, featv, out_ref, staged, own, ints, ints_in, sendp, recvp, wall, prm, wa, wb, w9, seg, im, im9, hid,
    sums, tsend, tin, tback, pad_in, pad_own, gpad, inv,
    small_sem, feat_sem, out_sem, int_s, int_r, pl_s, pl_r, w_s, w_r, p_s, p_r, a_s, a_r, b_s, b_r, c_s, c_r,
):
    m = lax.axis_index("member")
    v = lax.axis_index("vol")
    nxt = lax.rem(v + 1, slabs)
    prv = lax.rem(v + slabs - 1, slabs)
    mates = [lax.rem(m + d, M) for d in range(1, M)]
    froms = [lax.rem(m + M - d, M) for d in range(1, M)]
    rows = featv.shape[2]

    small = [
        pltpu.make_async_copy(src, dst, small_sem.at[i])
        for i, (src, dst) in enumerate((
            (cz_hbm, cz_ref), (cy_hbm, cy_ref), (cnt_hbm, cnt_ref), (w_hbm, w_ref), (gain_hbm, gain_ref),
            (shift_hbm, shift_ref), (segw_hbm, segw_ref), (segb_hbm, segb_ref)))
    ]
    for copy in small:
        copy.start()
    feat_copy = pltpu.make_async_copy(feat, featv, feat_sem)
    feat_copy.start()

    barrier = pltpu.get_barrier_semaphore()
    for target in [(m, nxt), (m, prv)] + [(mate, v) for mate in mates]:
        pl.semaphore_signal(barrier, inc=1, device_id=target, device_id_type=MESH)

    for copy in small:
        copy.wait()

    def chosen(ref_row):
        value = ref_row(0)
        for k in range(1, MAXP):
            value = jnp.where(m == k, ref_row(k), value)
        return value

    my_z = chosen(lambda k: cz_ref[0, k])
    my_y = chosen(lambda k: cy_ref[0, k])

    lane = lax.broadcasted_iota(jnp.int32, (8, X), 1)
    row = jnp.where(lane == 8, cnt_ref[0], 0)
    for k in range(MAXP):
        row = jnp.where(lane == k, cz_ref[0, k], row)
        row = jnp.where(lane == 4 + k, cy_ref[0, k], row)
    ints[...] = row

    for kz in range(3):
        for ky in range(3):
            for kx in range(3):
                from_y = jnp.where((m // 2) % 2 == 1, 2 - ky, ky)
                from_x = jnp.where(m % 2 == 1, 2 - kx, kx)
                tap = w_ref[kz, from_y, from_x]
                t = ky * 3 + kx
                at = kz * 256 + t * C if t < 8 else 768 + kz * C
                wall[m, :, at:at + C] = tap
    prm[m] = jnp.zeros((8, X), f32)
    prm[m, 0:1, 0:C] = gain_ref[...]
    prm[m, 1:2, 0:C] = shift_ref[...]
    prm[m, 2:5, 0:C] = segw_ref[0].astype(f32)
    prm[m, 5:6, 0:K] = segb_ref[...]

    pl.semaphore_wait(barrier, 2 + len(mates))

    int_copy = pltpu.make_async_remote_copy(
        src_ref=ints, dst_ref=ints_in, send_sem=int_s, recv_sem=int_r,
        device_id=(m, nxt), device_id_type=MESH)
    int_copy.start()

    def shared(buf, send, recv, d):
        return pltpu.make_async_remote_copy(
            src_ref=buf.at[m], dst_ref=buf.at[m], send_sem=send.at[d], recv_sem=recv.at[d],
            device_id=(mates[d], v), device_id_type=MESH)

    def arrives(buf, send, recv, d):
        return pltpu.make_async_remote_copy(
            src_ref=buf.at[froms[d]], dst_ref=buf.at[froms[d]], send_sem=send.at[d], recv_sem=recv.at[d],
            device_id=(mates[d], v), device_id_type=MESH)

    for d in range(M - 1):
        shared(wall, w_s, w_r, d).start()
        shared(prm, p_s, p_r, d).start()

    def plane_copy(j):
        return pltpu.make_async_remote_copy(
            src_ref=sendp.at[j], dst_ref=recvp.at[j], send_sem=pl_s.at[j], recv_sem=pl_r.at[j],
            device_id=(m, nxt), device_id_type=MESH)

    feat_copy.wait()
    for j in range(PZ):
        z = jnp.minimum(my_z + j, depth - 1)

        def stage(c, carry, z=z):
            staged[pl.ds(c * rows, rows), :] = featv[c, z].astype(f32)
            return carry

        lax.fori_loop(0, C, stage, 0, unroll=8)

        def pick(y, carry, j=j):
            sendp[j, y] = staged[pl.ds(my_y + y, C, stride=rows), :].astype(bf16)
            return carry

        lax.fori_loop(0, PY, pick, 0, unroll=4)
        plane_copy(j).start()

    inside = (v > 0).astype(f32)
    for j in range(PZ - 1):
        def stage(c, carry, j=j):
            own[pl.ds(j * C * rows + c * rows, rows), :] = featv[c, j].astype(f32) * inside
            return carry

        lax.fori_loop(0, C, stage, 0, unroll=8)

    for j in range(PZ):
        for kx in range(3):
            im[j * 256 + kx * C:j * 256 + (kx + 1) * C, X:2 * X] = jnp.zeros((C, X), bf16)
        for kx in range(2):
            t = 6 + kx
            im[j * 256 + t * C:j * 256 + (t + 1) * C, 8 * X:9 * X] = jnp.zeros((C, X), bf16)
        im9[j * C:(j + 1) * C, 8 * X:9 * X] = jnp.zeros((C, X), bf16)

    int_copy.wait_recv()
    got = ints_in[...]
    prev_z = [jnp.sum(jnp.where(lane[0:1] == k, got[0:1], 0)) for k in range(MAXP)]
    prev_y = [jnp.sum(jnp.where(lane[0:1] == 4 + k, got[0:1], 0)) for k in range(MAXP)]
    prev_count = jnp.sum(jnp.where(lane[0:1] == 8, got[0:1], 0))
    at_z = chosen(lambda k: prev_z[k])
    at_y = chosen(lambda k: prev_y[k])

    gz, gy = bell(PZ), bell(PY)
    gyx = picked(gy, lax.broadcasted_iota(jnp.int32, (PY, X), 0)) * bell_x((PY, X))
    nothing = jnp.zeros((PY, X), f32)
    for j in range(PZ + 2):
        gpad[j, 0:8] = nothing
        gpad[j, 16:24] = nothing
        gpad[j, 8:16] = nothing if j in (0, PZ + 1) else gyx * (gz[j - 1] * M)
    for pad in (pad_in, pad_own):
        for s in range(MAXP):
            for j in range(PZ + 2):
                for k in range(K - 1):
                    pad[s, j, k, 0:8] = nothing
                    pad[s, j, k, 16:24] = nothing
                    if j in (0, PZ + 1):
                        pad[s, j, k, 8:16] = nothing

    first = m * PY
    own_off = [8 + jnp.clip(first - cy_ref[0, k], -8, 8) for k in range(MAXP)]
    in_off = [8 + jnp.clip(first - prev_y[k], -8, 8) for k in range(MAXP)]
    own_live = [(k < cnt_ref[0]).astype(f32) for k in range(MAXP)]
    in_live = [((k < prev_count) & (v > 0)).astype(f32) for k in range(MAXP)]

    def which(z):
        return 1 + jnp.clip(z, -1, PZ)

    def weigh(z, carry):
        total = jnp.zeros((PY, X), f32)
        for k in range(MAXP):
            total = total + gpad[which(z - cz_ref[0, k]), pl.ds(own_off[k], 8), :] * own_live[k]
            total = total + gpad[which(z + depth - prev_z[k]), pl.ds(in_off[k], 8), :] * in_live[k]
        inv[z] = 1.0 / jnp.maximum(total, 0.1)
        return carry

    lax.fori_loop(0, depth, weigh, 0)

    for d in range(M - 1):
        arrives(wall, w_s, w_r, d).wait_recv()
        arrives(prm, p_s, p_r, d).wait_recv()
    wa[...] = jnp.zeros(wa.shape, bf16)
    wb[...] = jnp.zeros(wb.shape, bf16)
    w9[...] = jnp.zeros(w9.shape, bf16)
    for q in range(M):
        r = q * C
        full = wall[q, :, 0:768]
        wa[r:r + C, 0:512] = full[:, 256:768]
        wa[128 + r:128 + r + C, :] = full
        wb[r:r + C, :] = full
        wb[128 + r:128 + r + C, 256:768] = full[:, 0:512]
        for o in range(PZ):
            for kz in range(3):
                j = o + kz - 1
                if 0 <= j < PZ:
                    w9[o * 128 + r:o * 128 + r + C, j * C:(j + 1) * C] = wall[q, :, 768 + kz * C:768 + (kz + 1) * C]

    def column(values):
        eye = lax.broadcasted_iota(jnp.int32, (C, C), 0) == lax.broadcasted_iota(jnp.int32, (C, C), 1)
        return jnp.sum(jnp.where(eye, jnp.broadcast_to(values, (C, C)), 0.0), axis=1, keepdims=True)

    gain = jnp.concatenate([column(prm[q, 0:1, 0:C]) for q in range(M)], axis=0)
    shift = jnp.concatenate([column(prm[q, 1:2, 0:C]) for q in range(M)], axis=0)
    seg[...] = jnp.zeros(seg.shape, f32)
    for q in range(M):
        for o in range(2):
            at = o * 128 + q * C
            for k in range(K - 1):
                seg[k * 2 + o:k * 2 + o + 1, at:at + C] = prm[q, 2 + k:3 + k, 0:C]
                seg[8 + k * 2 + o:8 + k * 2 + o + 1, at:at + C] = prm[q, 4:5, 0:C]
    head = seg[...].astype(bf16)
    offsets = prm[0, 5:6, :] + prm[1, 5:6, :] + prm[2, 5:6, :] + prm[3, 5:6, :]
    offset = [jnp.sum(jnp.where(lane[0:1] == k, offsets, 0.0)) for k in range(K)]
    sub = lax.broadcasted_iota(jnp.int32, (8, 1), 0)
    bias = jnp.where(sub < 2, offset[0] - offset[2], offset[1] - offset[2])

    lane_row = lax.broadcasted_iota(jnp.int32, (C, X), 1)
    for j in range(PZ):
        plane_copy(j).wait_recv()
        beyond = at_z + j - depth
        start = jnp.clip(beyond, 0, PZ - 2) * (C * rows) + at_y

        def expand(y, carry, j=j, beyond=beyond, start=start):
            value = recvp[j, y].astype(f32)
            if j > 0:
                value = jnp.where(beyond >= 0, own[pl.ds(start + y, C, stride=rows), :], value)
            left = jnp.where(lane_row == 0, 0.0, pltpu.roll(value, 1, 1)).astype(bf16)
            right = jnp.where(lane_row == X - 1, 0.0, pltpu.roll(value, X - 1, 1)).astype(bf16)
            middle = value.astype(bf16)
            for ky in range(3):
                at = pl.ds(pl.multiple_of((y - ky + 2) * X, X), X)
                for kx, part in enumerate((left, middle, right)):
                    t = ky * 3 + kx
                    if t < 8:
                        im[j * 256 + t * C:j * 256 + (t + 1) * C, at] = part
                    else:
                        im9[j * C:(j + 1) * C, at] = part
            return carry

        lax.fori_loop(0, PY, expand, 0, unroll=2)

    sums[...] = jnp.zeros(sums.shape, f32)
    for p, taps in enumerate((wa, wb)):
        def conv(n, carry, p=p, taps=taps):
            at = pl.ds(pl.multiple_of(X + n * 256, X), 256)
            got = jnp.dot(taps[...], im[p * 256:p * 256 + 768, at], preferred_element_type=f32)
            got = got + jnp.dot(w9[p * 256:(p + 1) * 256, :], im9[:, at], preferred_element_type=f32)
            hid[p, :, pl.ds(pl.multiple_of(n * 256, 256), 256)] = got
            pair = got[:128] + got[128:]
            sums[...] += pair[:, :X] + pair[:, X:]
            return carry

        lax.fori_loop(0, 4, conv, 0)

    voxels = PZ * PY * X
    mean = jnp.sum(sums[...], axis=1, keepdims=True) / voxels
    sums[...] = jnp.zeros(sums.shape, f32)
    for p in range(2):
        def spread(n, carry, p=p):
            got = hid[p, :, pl.ds(pl.multiple_of(n * 256, 256), 256)]
            low = got[:128] - mean
            high = got[128:] - mean
            pair = low * low + high * high
            sums[...] += pair[:, :X] + pair[:, X:]
            return carry

        lax.fori_loop(0, 4, spread, 0)
    variance = jnp.sum(sums[...], axis=1, keepdims=True) / voxels
    scale = lax.rsqrt(variance + 1e-05) * gain

    alive = m < prev_count
    gx = bell_x((8, X))
    for p in range(2):
        gzp = jnp.where(sub % 2 == 0, f32(gz[2 * p]), f32(gz[2 * p + 1]))

        def classify(n, carry, p=p, gzp=gzp):
            parts = []
            for o in range(2):
                got = hid[p, o * 128:(o + 1) * 128, pl.ds(pl.multiple_of(n * 256, 256), 256)]
                normed = (got - mean) * scale + shift
                parts.append(jnp.maximum(normed, 0.01 * normed).astype(bf16))
            act = jnp.concatenate(parts, axis=0)
            both = jnp.dot(head, act, preferred_element_type=f32)
            logit = both[0:8] - both[8:16] + bias
            for h in range(2):
                y = n * 2 + h
                gyv = f32(gy[0])
                for i in range(1, PY):
                    gyv = jnp.where(y == i, f32(gy[i]), gyv)
                value = logit[:, h * X:(h + 1) * X] * (gx * gzp * gyv)
                value = jnp.where(alive, value, 0.0)
                tsend[p, pl.ds(y, 8, stride=8), :] = value
            return carry

        lax.fori_loop(0, 4, classify, 0)

    back = pltpu.make_async_remote_copy(
        src_ref=tsend.at[:, pl.ds(0, 32)], dst_ref=tback.at[m], send_sem=b_s, recv_sem=b_r,
        device_id=(m, prv), device_id_type=MESH)
    back.start()

    def across(d):
        return pltpu.make_async_remote_copy(
            src_ref=tsend.at[:, pl.ds(0, 32)], dst_ref=tin.at[m], send_sem=a_s.at[d], recv_sem=a_r.at[d],
            device_id=(mates[d], v), device_id_type=MESH)

    for d in range(M - 1):
        across(d).start()
    back.wait_recv()
    for d in range(M - 1):
        shared(tback, c_s, c_r, d).start()
    tin[m] = tsend[:, 0:32]

    def spread_out(buf, pad, s):
        for p in range(2):
            for k in range(K - 1):
                for o in range(2):
                    r = (k * 2 + o) * 8
                    pad[s, 1 + 2 * p + o, k, 8:16] = buf[s, p, r:r + 8]

    for d in range(M - 1):
        arrives(tin, a_s, a_r, d).wait_recv()
    for s in range(MAXP):
        spread_out(tin, pad_in, s)
    for d in range(M - 1):
        arrives(tback, c_s, c_r, d).wait_recv()
    for s in range(MAXP):
        spread_out(tback, pad_own, s)

    def finish(z, spill):
        diff = []
        for k in range(K - 1):
            total = jnp.zeros((PY, X), f32)
            for s in range(MAXP):
                total = total + pad_own[s, which(z - cz_ref[0, s]), k, pl.ds(own_off[s], 8), :]
                if spill:
                    total = total + pad_in[s, which(z + depth - prev_z[s]), k, pl.ds(in_off[s], 8), :] * inside
            diff.append(total * inv[z])
        top = jnp.maximum(jnp.maximum(diff[0], diff[1]), 0.0)
        powers = [jnp.exp(diff[0] - top), jnp.exp(diff[1] - top), jnp.exp(-top)]
        whole = 1.0 / (powers[0] + powers[1] + powers[2])
        for k in range(K):
            out_ref[k, z] = powers[k] * whole

    def rest(z, carry):
        finish(z, False)
        return carry

    group = depth // 4
    outs = [
        pltpu.make_async_copy(
            out_ref.at[:, pl.ds(g * group, group)], out_hbm.at[:, pl.ds(g * group, group)], out_sem.at[g])
        for g in range(4)
    ]
    for z in range(PZ - 1):
        finish(z, True)
    for g in range(4):
        lax.fori_loop(max(g * group, PZ - 1), (g + 1) * group, rest, 0)
        outs[g].start()

    for copy in outs:
        copy.wait()
    int_copy.wait_send()
    for j in range(PZ):
        plane_copy(j).wait_send()
    back.wait_send()
    for d in range(M - 1):
        shared(wall, w_s, w_r, d).wait_send()
        shared(prm, p_s, p_r, d).wait_send()
        across(d).wait_send()
        shared(tback, c_s, c_r, d).wait_send()


def per_device(slabs, features, corner_z, corner_y, counts, conv_w, norm_gain, norm_shift, seg_w, seg_b):
    channels, depth, rows, width = features.shape
    taps = conv_w[0].transpose(2, 3, 4, 0, 1)
    dma = pltpu.SemaphoreType.DMA
    return pl.pallas_call(
        functools.partial(kernel, depth, slabs),
        name="ensemble_patches",
        out_shape=pltpu.HBM((K, depth, rows // M, width), f32),
        in_specs=[pl.BlockSpec(memory_space=pltpu.HBM)] * 9,
        out_specs=pl.BlockSpec(memory_space=pltpu.HBM),
        scratch_shapes=[
            pltpu.SMEM((1, MAXP), jnp.int32),
            pltpu.SMEM((1, MAXP), jnp.int32),
            pltpu.SMEM((1,), jnp.int32),
            pltpu.VMEM((3, 3, 3, C, C), bf16),
            pltpu.VMEM((1, C), f32),
            pltpu.VMEM((1, C), f32),
            pltpu.VMEM((1, K, C), bf16),
            pltpu.VMEM((1, K), f32),
            pltpu.VMEM((channels, depth, rows, width), bf16),
            pltpu.VMEM((K, depth, rows // M, width), f32),
            pltpu.VMEM((C * rows, X), f32),
            pltpu.VMEM(((PZ - 1) * C * rows, X), f32),
            pltpu.VMEM((8, X), jnp.int32),
            pltpu.VMEM((8, X), jnp.int32),
            pltpu.VMEM((PZ, PY, C, X), bf16),
            pltpu.VMEM((PZ, PY, C, X), bf16),
            pltpu.VMEM((M, C, 896), bf16),
            pltpu.VMEM((M, 8, X), f32),
            pltpu.VMEM((256, 768), bf16),
            pltpu.VMEM((256, 768), bf16),
            pltpu.VMEM((512, 128), bf16),
            pltpu.VMEM((16, 256), f32),
            pltpu.VMEM((PZ * 256, 10 * X), bf16),
            pltpu.VMEM((PZ * C, 10 * X), bf16),
            pltpu.VMEM((2, 256, PY * X), f32),
            pltpu.VMEM((128, X), f32),
            pltpu.VMEM((2, 64, X), f32),
            pltpu.VMEM((M, 2, 32, X), f32),
            pltpu.VMEM((M, 2, 32, X), f32),
            pltpu.VMEM((MAXP, PZ + 2, K - 1, 24, X), f32),
            pltpu.VMEM((MAXP, PZ + 2, K - 1, 24, X), f32),
            pltpu.VMEM((PZ + 2, 24, X), f32),
            pltpu.VMEM((depth, PY, X), f32),
            dma((8,)), dma, dma((4,)), dma, dma, dma((PZ,)), dma((PZ,)), dma((3,)), dma((3,)), dma((3,)), dma((3,)),
            dma((3,)), dma((3,)), dma, dma, dma((3,)), dma((3,)),
        ],
        compiler_params=pltpu.CompilerParams(
            collective_id=0, has_side_effects=True, vmem_limit_bytes=40 * 1024 * 1024),
    )(*[
        arg if arg is counts else pltpu.with_memory_space_constraint(arg, pltpu.HBM)
        for arg in (features, corner_z, corner_y, counts, taps, norm_gain, norm_shift, seg_w, seg_b)])


def solution(mesh):
    placed = (
        P(None, "vol", None, None),
        P("vol", None),
        P("vol", None),
        P("vol"),
        P("member", None, None, None, None, None),
        P("member", None),
        P("member", None),
        P("member", None, None),
        P("member", None),
    )
    return jax.shard_map(
        functools.partial(per_device, mesh.shape["vol"]),
        mesh=mesh,
        in_specs=placed,
        out_specs=P(None, "vol", "member", None),
        check_vma=False,
    )
```

```python
import functools

import jax
import jax.numpy as jnp
import numpy as np
from jax import lax
from jax.experimental import pallas as pl
from jax.experimental.pallas import tpu as pltpu
from jax.sharding import PartitionSpec as P

MESH = pl.DeviceIdType.MESH
C = 32
K = 3
PZ = 4
PY = 8
X = 128
MAXP = 4
M = 4
f32 = jnp.float32
bf16 = jnp.bfloat16


def bell(length):
    position = np.arange(length, dtype=np.float64)
    center = (length - 1) / 2.0
    sigma = length / 4.0
    return [float(v) for v in np.exp(-((position - center) ** 2) / (2.0 * sigma * sigma))]


def bell_x(shape):
    position = lax.broadcasted_iota(jnp.int32, shape, len(shape) - 1).astype(f32)
    center = (X - 1) / 2.0
    sigma = X / 4.0
    return jnp.exp(-((position - center) ** 2) / (2.0 * sigma * sigma))


def picked(values, index):
    out = jnp.full(index.shape, values[0], f32)
    for i in range(1, len(values)):
        out = jnp.where(index == i, f32(values[i]), out)
    return out


def kernel(
    depth, slabs,
    feat, cz_hbm, cy_hbm, cnt_hbm, w_hbm, gain_hbm, shift_hbm, segw_hbm, segb_hbm,
    out_ref,
    cz_ref, cy_ref, cnt_ref, w_ref, gain_ref, shift_ref, segw_ref, segb_ref, featv, staged, own, ints, ints_in, sendp, recvp, wall, prm, wa, wb, w9, seg, im, im9, hid,
    sums, tsend, tin, tback, pad_in, pad_own, gpad, inv,
    small_sem, feat_sem, int_s, int_r, pl_s, pl_r, w_s, w_r, p_s, p_r, a_s, a_r, b_s, b_r, c_s, c_r,
):
    m = lax.axis_index("member")
    v = lax.axis_index("vol")
    nxt = lax.rem(v + 1, slabs)
    prv = lax.rem(v + slabs - 1, slabs)
    mates = [lax.rem(m + d, M) for d in range(1, M)]
    froms = [lax.rem(m + M - d, M) for d in range(1, M)]
    rows = featv.shape[2]

    small = [
        pltpu.make_async_copy(src, dst, small_sem.at[i])
        for i, (src, dst) in enumerate((
            (cz_hbm, cz_ref), (cy_hbm, cy_ref), (cnt_hbm, cnt_ref), (w_hbm, w_ref), (gain_hbm, gain_ref),
            (shift_hbm, shift_ref), (segw_hbm, segw_ref), (segb_hbm, segb_ref)))
    ]
    for copy in small:
        copy.start()
    feat_copy = pltpu.make_async_copy(feat, featv, feat_sem)
    feat_copy.start()

    barrier = pltpu.get_barrier_semaphore()
    for target in [(m, nxt), (m, prv)] + [(mate, v) for mate in mates]:
        pl.semaphore_signal(barrier, inc=1, device_id=target, device_id_type=MESH)

    for copy in small:
        copy.wait()

    def chosen(ref_row):
        value = ref_row(0)
        for k in range(1, MAXP):
            value = jnp.where(m == k, ref_row(k), value)
        return value

    my_z = chosen(lambda k: cz_ref[0, k])
    my_y = chosen(lambda k: cy_ref[0, k])

    lane = lax.broadcasted_iota(jnp.int32, (8, X), 1)
    row = jnp.where(lane == 8, cnt_ref[0], 0)
    for k in range(MAXP):
        row = jnp.where(lane == k, cz_ref[0, k], row)
        row = jnp.where(lane == 4 + k, cy_ref[0, k], row)
    ints[...] = row

    for kz in range(3):
        for ky in range(3):
            for kx in range(3):
                from_y = jnp.where((m // 2) % 2 == 1, 2 - ky, ky)
                from_x = jnp.where(m % 2 == 1, 2 - kx, kx)
                tap = w_ref[kz, from_y, from_x]
                t = ky * 3 + kx
                at = kz * 256 + t * C if t < 8 else 768 + kz * C
                wall[m, :, at:at + C] = tap
    prm[m] = jnp.zeros((8, X), f32)
    prm[m, 0:1, 0:C] = gain_ref[...]
    prm[m, 1:2, 0:C] = shift_ref[...]
    prm[m, 2:5, 0:C] = segw_ref[0].astype(f32)
    prm[m, 5:6, 0:K] = segb_ref[...]

    for j in range(PZ):
        for kx in range(3):
            im[j * 256 + kx * C:j * 256 + (kx + 1) * C, X:2 * X] = jnp.zeros((C, X), bf16)
        for kx in range(2):
            t = 6 + kx
            im[j * 256 + t * C:j * 256 + (t + 1) * C, 8 * X:9 * X] = jnp.zeros((C, X), bf16)
        im9[j * C:(j + 1) * C, 8 * X:9 * X] = jnp.zeros((C, X), bf16)

    gz, gy = bell(PZ), bell(PY)
    gyx = picked(gy, lax.broadcasted_iota(jnp.int32, (PY, X), 0)) * bell_x((PY, X))
    nothing = jnp.zeros((PY, X), f32)
    for j in range(PZ + 2):
        gpad[j, 0:8] = nothing
        gpad[j, 16:24] = nothing
        gpad[j, 8:16] = nothing if j in (0, PZ + 1) else gyx * (gz[j - 1] * M)
    for pad in (pad_in, pad_own):
        for s in range(MAXP):
            for j in range(PZ + 2):
                for k in range(K - 1):
                    pad[s, j, k, 0:8] = nothing
                    pad[s, j, k, 16:24] = nothing
                    if j in (0, PZ + 1):
                        pad[s, j, k, 8:16] = nothing
    wa[...] = jnp.zeros(wa.shape, bf16)
    wb[...] = jnp.zeros(wb.shape, bf16)
    w9[...] = jnp.zeros(w9.shape, bf16)
    seg[...] = jnp.zeros(seg.shape, f32)

    pl.semaphore_wait(barrier, 2 + len(mates))

    int_copy = pltpu.make_async_remote_copy(
        src_ref=ints, dst_ref=ints_in, send_sem=int_s, recv_sem=int_r,
        device_id=(m, nxt), device_id_type=MESH)
    int_copy.start()

    def shared(buf, send, recv, d):
        return pltpu.make_async_remote_copy(
            src_ref=buf.at[m], dst_ref=buf.at[m], send_sem=send.at[d], recv_sem=recv.at[d],
            device_id=(mates[d], v), device_id_type=MESH)

    def arrives(buf, send, recv, d):
        return pltpu.make_async_remote_copy(
            src_ref=buf.at[froms[d]], dst_ref=buf.at[froms[d]], send_sem=send.at[d], recv_sem=recv.at[d],
            device_id=(mates[d], v), device_id_type=MESH)

    for d in range(M - 1):
        shared(wall, w_s, w_r, d).start()
        shared(prm, p_s, p_r, d).start()

    def plane_copy(j):
        return pltpu.make_async_remote_copy(
            src_ref=sendp.at[j], dst_ref=recvp.at[j], send_sem=pl_s.at[j], recv_sem=pl_r.at[j],
            device_id=(m, nxt), device_id_type=MESH)

    feat_copy.wait()
    for j in range(PZ):
        z = jnp.minimum(my_z + j, depth - 1)

        def stage(c, carry, z=z):
            staged[pl.ds(c * rows, rows), :] = featv[c, z].astype(f32)
            return carry

        lax.fori_loop(0, C, stage, 0, unroll=8)

        def pick(y, carry, j=j):
            sendp[j, y] = staged[pl.ds(my_y + y, C, stride=rows), :].astype(bf16)
            return carry

        lax.fori_loop(0, PY, pick, 0, unroll=4)
        plane_copy(j).start()

    inside = (v > 0).astype(f32)
    for j in range(PZ - 1):
        def stage(c, carry, j=j):
            own[pl.ds(j * C * rows + c * rows, rows), :] = featv[c, j].astype(f32) * inside
            return carry

        lax.fori_loop(0, C, stage, 0, unroll=8)

    int_copy.wait_recv()
    got = ints_in[...]
    prev_z = [jnp.sum(jnp.where(lane[0:1] == k, got[0:1], 0)) for k in range(MAXP)]
    prev_y = [jnp.sum(jnp.where(lane[0:1] == 4 + k, got[0:1], 0)) for k in range(MAXP)]
    prev_count = jnp.sum(jnp.where(lane[0:1] == 8, got[0:1], 0))
    at_z = chosen(lambda k: prev_z[k])
    at_y = chosen(lambda k: prev_y[k])

    first = m * PY
    own_off = [8 + jnp.clip(first - cy_ref[0, k], -8, 8) for k in range(MAXP)]
    in_off = [8 + jnp.clip(first - prev_y[k], -8, 8) for k in range(MAXP)]
    own_live = [(k < cnt_ref[0]).astype(f32) for k in range(MAXP)]
    in_live = [((k < prev_count) & (v > 0)).astype(f32) for k in range(MAXP)]

    def which(z):
        return 1 + jnp.clip(z, -1, PZ)

    def weigh(z, carry):
        total = jnp.zeros((PY, X), f32)
        for k in range(MAXP):
            total = total + gpad[which(z - cz_ref[0, k]), pl.ds(own_off[k], 8), :] * own_live[k]
            total = total + gpad[which(z + depth - prev_z[k]), pl.ds(in_off[k], 8), :] * in_live[k]
        inv[z] = 1.0 / jnp.maximum(total, 0.1)
        return carry

    lax.fori_loop(0, depth, weigh, 0, unroll=4)

    for d in range(M - 1):
        arrives(wall, w_s, w_r, d).wait_recv()
        arrives(prm, p_s, p_r, d).wait_recv()
    for q in range(M):
        r = q * C
        full = wall[q, :, 0:768]
        wa[r:r + C, 0:512] = full[:, 256:768]
        wa[128 + r:128 + r + C, :] = full
        wb[r:r + C, :] = full
        wb[128 + r:128 + r + C, 256:768] = full[:, 0:512]
        for o in range(PZ):
            for kz in range(3):
                j = o + kz - 1
                if 0 <= j < PZ:
                    w9[o * 128 + r:o * 128 + r + C, j * C:(j + 1) * C] = wall[q, :, 768 + kz * C:768 + (kz + 1) * C]

    def column(values):
        eye = lax.broadcasted_iota(jnp.int32, (C, C), 0) == lax.broadcasted_iota(jnp.int32, (C, C), 1)
        return jnp.sum(jnp.where(eye, jnp.broadcast_to(values, (C, C)), 0.0), axis=1, keepdims=True)

    gain = jnp.concatenate([column(prm[q, 0:1, 0:C]) for q in range(M)], axis=0)
    shift = jnp.concatenate([column(prm[q, 1:2, 0:C]) for q in range(M)], axis=0)
    for q in range(M):
        for o in range(2):
            at = o * 128 + q * C
            for k in range(K - 1):
                seg[k * 2 + o:k * 2 + o + 1, at:at + C] = prm[q, 2 + k:3 + k, 0:C]
                seg[8 + k * 2 + o:8 + k * 2 + o + 1, at:at + C] = prm[q, 4:5, 0:C]
    head = seg[...].astype(bf16)
    offsets = prm[0, 5:6, :] + prm[1, 5:6, :] + prm[2, 5:6, :] + prm[3, 5:6, :]
    offset = [jnp.sum(jnp.where(lane[0:1] == k, offsets, 0.0)) for k in range(K)]
    sub = lax.broadcasted_iota(jnp.int32, (8, 1), 0)
    bias = jnp.where(sub < 2, offset[0] - offset[2], offset[1] - offset[2])

    lane_row = lax.broadcasted_iota(jnp.int32, (C, X), 1)
    for j in range(PZ):
        plane_copy(j).wait_recv()
        beyond = at_z + j - depth
        start = jnp.clip(beyond, 0, PZ - 2) * (C * rows) + at_y

        def expand(y, carry, j=j, beyond=beyond, start=start):
            value = recvp[j, y].astype(f32)
            if j > 0:
                value = jnp.where(beyond >= 0, own[pl.ds(start + y, C, stride=rows), :], value)
            left = jnp.where(lane_row == 0, 0.0, pltpu.roll(value, 1, 1)).astype(bf16)
            right = jnp.where(lane_row == X - 1, 0.0, pltpu.roll(value, X - 1, 1)).astype(bf16)
            middle = value.astype(bf16)
            for ky in range(3):
                at = pl.ds(pl.multiple_of((y - ky + 2) * X, X), X)
                for kx, part in enumerate((left, middle, right)):
                    t = ky * 3 + kx
                    if t < 8:
                        im[j * 256 + t * C:j * 256 + (t + 1) * C, at] = part
                    else:
                        im9[j * C:(j + 1) * C, at] = part
            return carry

        lax.fori_loop(0, PY, expand, 0, unroll=2)

    sums[...] = jnp.zeros(sums.shape, f32)
    for p, taps in enumerate((wa, wb)):
        def conv(n, carry, p=p, taps=taps):
            at = pl.ds(pl.multiple_of(X + n * 256, X), 256)
            got = jnp.dot(taps[...], im[p * 256:p * 256 + 768, at], preferred_element_type=f32)
            got = got + jnp.dot(w9[p * 256:(p + 1) * 256, :], im9[:, at], preferred_element_type=f32)
            hid[p, :, pl.ds(pl.multiple_of(n * 256, 256), 256)] = got
            pair = got[:128] + got[128:]
            sums[...] += pair[:, :X] + pair[:, X:]
            return carry

        lax.fori_loop(0, 4, conv, 0, unroll=True)

    voxels = PZ * PY * X
    mean = jnp.sum(sums[...], axis=1, keepdims=True) / voxels
    sums[...] = jnp.zeros(sums.shape, f32)
    for p in range(2):
        def spread(n, carry, p=p):
            got = hid[p, :, pl.ds(pl.multiple_of(n * 256, 256), 256)]
            low = got[:128] - mean
            high = got[128:] - mean
            pair = low * low + high * high
            sums[...] += pair[:, :X] + pair[:, X:]
            return carry

        lax.fori_loop(0, 4, spread, 0, unroll=True)
    variance = jnp.sum(sums[...], axis=1, keepdims=True) / voxels
    scale = lax.rsqrt(variance + 1e-05) * gain

    alive = m < prev_count
    gx = bell_x((8, X))
    for p in range(2):
        gzp = jnp.where(sub % 2 == 0, f32(gz[2 * p]), f32(gz[2 * p + 1]))

        def classify(n, carry, p=p, gzp=gzp):
            parts = []
            for o in range(2):
                got = hid[p, o * 128:(o + 1) * 128, pl.ds(pl.multiple_of(n * 256, 256), 256)]
                normed = (got - mean) * scale + shift
                parts.append(jnp.maximum(normed, 0.01 * normed).astype(bf16))
            act = jnp.concatenate(parts, axis=0)
            both = jnp.dot(head, act, preferred_element_type=f32)
            logit = both[0:8] - both[8:16] + bias
            for h in range(2):
                y = n * 2 + h
                gyv = f32(gy[0])
                for i in range(1, PY):
                    gyv = jnp.where(y == i, f32(gy[i]), gyv)
                value = logit[:, h * X:(h + 1) * X] * (gx * gzp * gyv)
                value = jnp.where(alive, value, 0.0)
                tsend[p, pl.ds(y, 8, stride=8), :] = value
            return carry

        lax.fori_loop(0, 4, classify, 0, unroll=True)

    back = pltpu.make_async_remote_copy(
        src_ref=tsend.at[:, pl.ds(0, 32)], dst_ref=tback.at[m], send_sem=b_s, recv_sem=b_r,
        device_id=(m, prv), device_id_type=MESH)
    back.start()

    def across(d):
        return pltpu.make_async_remote_copy(
            src_ref=tsend.at[:, pl.ds(0, 32)], dst_ref=tin.at[m], send_sem=a_s.at[d], recv_sem=a_r.at[d],
            device_id=(mates[d], v), device_id_type=MESH)

    for d in range(M - 1):
        across(d).start()
    back.wait_recv()
    for d in range(M - 1):
        shared(tback, c_s, c_r, d).start()
    tin[m] = tsend[:, 0:32]

    def spread_out(buf, pad, s):
        for p in range(2):
            for k in range(K - 1):
                for o in range(2):
                    r = (k * 2 + o) * 8
                    pad[s, 1 + 2 * p + o, k, 8:16] = buf[s, p, r:r + 8]

    for d in range(M - 1):
        arrives(tin, a_s, a_r, d).wait_recv()
    for s in range(MAXP):
        spread_out(tin, pad_in, s)
    for d in range(M - 1):
        arrives(tback, c_s, c_r, d).wait_recv()
    for s in range(MAXP):
        spread_out(tback, pad_own, s)

    def finish(z, spill):
        diff = []
        for k in range(K - 1):
            total = jnp.zeros((PY, X), f32)
            for s in range(MAXP):
                total = total + pad_own[s, which(z - cz_ref[0, s]), k, pl.ds(own_off[s], 8), :]
                if spill:
                    total = total + pad_in[s, which(z + depth - prev_z[s]), k, pl.ds(in_off[s], 8), :] * inside
            diff.append(total * inv[z])
        top = jnp.maximum(jnp.maximum(diff[0], diff[1]), 0.0)
        powers = [jnp.exp(diff[0] - top), jnp.exp(diff[1] - top), jnp.exp(-top)]
        whole = 1.0 / (powers[0] + powers[1] + powers[2])
        for k in range(K):
            out_ref[k, z] = powers[k] * whole

    def rest(z, carry):
        finish(z, False)
        return carry

    for z in range(PZ - 1):
        finish(z, True)
    lax.fori_loop(PZ - 1, depth, rest, 0, unroll=True)

    int_copy.wait_send()
    for j in range(PZ):
        plane_copy(j).wait_send()
    back.wait_send()
    for d in range(M - 1):
        shared(wall, w_s, w_r, d).wait_send()
        shared(prm, p_s, p_r, d).wait_send()
        across(d).wait_send()
        shared(tback, c_s, c_r, d).wait_send()


def per_device(slabs, features, corner_z, corner_y, counts, conv_w, norm_gain, norm_shift, seg_w, seg_b):
    channels, depth, rows, width = features.shape
    taps = conv_w[0].transpose(2, 3, 4, 0, 1)
    dma = pltpu.SemaphoreType.DMA
    return pl.pallas_call(
        functools.partial(kernel, depth, slabs),
        name="ensemble_patches",
        out_shape=jax.ShapeDtypeStruct((K, depth, rows // M, width), f32),
        in_specs=[pl.BlockSpec(memory_space=pltpu.HBM)] * 9,
        out_specs=pl.BlockSpec(memory_space=pltpu.VMEM),
        scratch_shapes=[
            pltpu.SMEM((1, MAXP), jnp.int32),
            pltpu.SMEM((1, MAXP), jnp.int32),
            pltpu.SMEM((1,), jnp.int32),
            pltpu.VMEM((3, 3, 3, C, C), bf16),
            pltpu.VMEM((1, C), f32),
            pltpu.VMEM((1, C), f32),
            pltpu.VMEM((1, K, C), bf16),
            pltpu.VMEM((1, K), f32),
            pltpu.VMEM((channels, depth, rows, width), bf16),
            pltpu.VMEM((C * rows, X), f32),
            pltpu.VMEM(((PZ - 1) * C * rows, X), f32),
            pltpu.VMEM((8, X), jnp.int32),
            pltpu.VMEM((8, X), jnp.int32),
            pltpu.VMEM((PZ, PY, C, X), bf16),
            pltpu.VMEM((PZ, PY, C, X), bf16),
            pltpu.VMEM((M, C, 896), bf16),
            pltpu.VMEM((M, 8, X), f32),
            pltpu.VMEM((256, 768), bf16),
            pltpu.VMEM((256, 768), bf16),
            pltpu.VMEM((512, 128), bf16),
            pltpu.VMEM((16, 256), f32),
            pltpu.VMEM((PZ * 256, 10 * X), bf16),
            pltpu.VMEM((PZ * C, 10 * X), bf16),
            pltpu.VMEM((2, 256, PY * X), f32),
            pltpu.VMEM((128, X), f32),
            pltpu.VMEM((2, 64, X), f32),
            pltpu.VMEM((M, 2, 32, X), f32),
            pltpu.VMEM((M, 2, 32, X), f32),
            pltpu.VMEM((MAXP, PZ + 2, K - 1, 24, X), f32),
            pltpu.VMEM((MAXP, PZ + 2, K - 1, 24, X), f32),
            pltpu.VMEM((PZ + 2, 24, X), f32),
            pltpu.VMEM((depth, PY, X), f32),
            dma((8,)), dma, dma, dma, dma((PZ,)), dma((PZ,)), dma((3,)), dma((3,)), dma((3,)), dma((3,)),
            dma((3,)), dma((3,)), dma, dma, dma((3,)), dma((3,)),
        ],
        compiler_params=pltpu.CompilerParams(
            collective_id=0, has_side_effects=True, vmem_limit_bytes=40 * 1024 * 1024),
    )(*[
        arg if arg is counts else pltpu.with_memory_space_constraint(arg, pltpu.HBM)
        for arg in (features, corner_z, corner_y, counts, taps, norm_gain, norm_shift, seg_w, seg_b)])


def solution(mesh):
    placed = (
        P(None, "vol", None, None),
        P("vol", None),
        P("vol", None),
        P("vol"),
        P("member", None, None, None, None, None),
        P("member", None),
        P("member", None),
        P("member", None, None),
        P("member", None),
    )
    return jax.shard_map(
        functools.partial(per_device, mesh.shape["vol"]),
        mesh=mesh,
        in_specs=placed,
        out_specs=P(None, "vol", "member", None),
        check_vma=False,
    )
```

```python
import functools

import jax
import jax.numpy as jnp
import numpy as np
from jax import lax
from jax.experimental import pallas as pl
from jax.experimental.pallas import tpu as pltpu
from jax.sharding import PartitionSpec as P

MESH = pl.DeviceIdType.MESH
C = 32
K = 3
PZ = 4
PY = 8
X = 128
MAXP = 4
M = 4
f32 = jnp.float32
bf16 = jnp.bfloat16


def bell(length):
    position = np.arange(length, dtype=np.float64)
    center = (length - 1) / 2.0
    sigma = length / 4.0
    return [float(v) for v in np.exp(-((position - center) ** 2) / (2.0 * sigma * sigma))]


def bell_x(shape):
    position = lax.broadcasted_iota(jnp.int32, shape, len(shape) - 1).astype(f32)
    center = (X - 1) / 2.0
    sigma = X / 4.0
    return jnp.exp(-((position - center) ** 2) / (2.0 * sigma * sigma))


def picked(values, index):
    out = jnp.full(index.shape, values[0], f32)
    for i in range(1, len(values)):
        out = jnp.where(index == i, f32(values[i]), out)
    return out


def kernel(
    depth, slabs,
    feat, cz_hbm, cy_hbm, cnt_hbm, w_hbm, gain_hbm, shift_hbm, segw_hbm, segb_hbm,
    out_ref,
    cz_ref, cy_ref, cnt_ref, w_ref, gain_ref, shift_ref, segw_ref, segb_ref, featv, staged, own, ints, ints_in, sendp, recvp, wall, prm, wa, wb, w9, seg, im, im9, hid,
    sums, tsend, tin, tback, pad_in, pad_own, gpad, inv,
    small_sem, feat_sem, int_s, int_r, pl_s, pl_r, w_s, w_r, p_s, p_r, a_s, a_r, b_s, b_r, c_s, c_r,
):
    m = lax.axis_index("member")
    v = lax.axis_index("vol")
    nxt = lax.rem(v + 1, slabs)
    prv = lax.rem(v + slabs - 1, slabs)
    mates = [lax.rem(m + d, M) for d in range(1, M)]
    froms = [lax.rem(m + M - d, M) for d in range(1, M)]
    rows = featv.shape[2]

    small = [
        pltpu.make_async_copy(src, dst, small_sem.at[i])
        for i, (src, dst) in enumerate((
            (cz_hbm, cz_ref), (cy_hbm, cy_ref), (cnt_hbm, cnt_ref), (w_hbm, w_ref), (gain_hbm, gain_ref),
            (shift_hbm, shift_ref), (segw_hbm, segw_ref), (segb_hbm, segb_ref)))
    ]
    for copy in small:
        copy.start()
    feat_copy = pltpu.make_async_copy(feat, featv, feat_sem)
    feat_copy.start()

    barrier = pltpu.get_barrier_semaphore()
    for target in [(m, nxt), (m, prv)] + [(mate, v) for mate in mates]:
        pl.semaphore_signal(barrier, inc=1, device_id=target, device_id_type=MESH)

    for copy in small:
        copy.wait()

    def chosen(ref_row):
        value = ref_row(0)
        for k in range(1, MAXP):
            value = jnp.where(m == k, ref_row(k), value)
        return value

    my_z = chosen(lambda k: cz_ref[0, k])
    my_y = chosen(lambda k: cy_ref[0, k])

    lane = lax.broadcasted_iota(jnp.int32, (8, X), 1)
    row = jnp.where(lane == 8, cnt_ref[0], 0)
    for k in range(MAXP):
        row = jnp.where(lane == k, cz_ref[0, k], row)
        row = jnp.where(lane == 4 + k, cy_ref[0, k], row)
    ints[...] = row

    for kz in range(3):
        for ky in range(3):
            for kx in range(3):
                from_y = jnp.where((m // 2) % 2 == 1, 2 - ky, ky)
                from_x = jnp.where(m % 2 == 1, 2 - kx, kx)
                tap = w_ref[kz, from_y, from_x]
                t = ky * 3 + kx
                at = kz * 256 + t * C if t < 8 else 768 + kz * C
                wall[m, :, at:at + C] = tap
    prm[m] = jnp.zeros((8, X), f32)
    prm[m, 0:1, 0:C] = gain_ref[...]
    prm[m, 1:2, 0:C] = shift_ref[...]
    prm[m, 2:5, 0:C] = segw_ref[0].astype(f32)
    prm[m, 5:6, 0:K] = segb_ref[...]

    for j in range(PZ):
        for kx in range(3):
            im[j * 256 + kx * C:j * 256 + (kx + 1) * C, X:2 * X] = jnp.zeros((C, X), bf16)
        for kx in range(2):
            t = 6 + kx
            im[j * 256 + t * C:j * 256 + (t + 1) * C, 8 * X:9 * X] = jnp.zeros((C, X), bf16)
        im9[j * C:(j + 1) * C, 8 * X:9 * X] = jnp.zeros((C, X), bf16)

    gz, gy = bell(PZ), bell(PY)
    gyx = picked(gy, lax.broadcasted_iota(jnp.int32, (PY, X), 0)) * bell_x((PY, X))
    nothing = jnp.zeros((PY, X), f32)
    for j in range(PZ + 2):
        gpad[j, 0:8] = nothing
        gpad[j, 16:24] = nothing
        gpad[j, 8:16] = nothing if j in (0, PZ + 1) else gyx * (gz[j - 1] * M)
    for pad in (pad_in, pad_own):
        for s in range(MAXP):
            for j in range(PZ + 2):
                for k in range(K - 1):
                    pad[s, j, k, 0:8] = nothing
                    pad[s, j, k, 16:24] = nothing
                    if j in (0, PZ + 1):
                        pad[s, j, k, 8:16] = nothing
    wa[...] = jnp.zeros(wa.shape, bf16)
    wb[...] = jnp.zeros(wb.shape, bf16)
    w9[...] = jnp.zeros(w9.shape, bf16)
    seg[...] = jnp.zeros(seg.shape, f32)

    pl.semaphore_wait(barrier, 2 + len(mates))

    int_copy = pltpu.make_async_remote_copy(
        src_ref=ints, dst_ref=ints_in, send_sem=int_s, recv_sem=int_r,
        device_id=(m, nxt), device_id_type=MESH)
    int_copy.start()

    def shared(buf, send, recv, d):
        return pltpu.make_async_remote_copy(
            src_ref=buf.at[m], dst_ref=buf.at[m], send_sem=send.at[d], recv_sem=recv.at[d],
            device_id=(mates[d], v), device_id_type=MESH)

    def arrives(buf, send, recv, d):
        return pltpu.make_async_remote_copy(
            src_ref=buf.at[froms[d]], dst_ref=buf.at[froms[d]], send_sem=send.at[d], recv_sem=recv.at[d],
            device_id=(mates[d], v), device_id_type=MESH)

    for d in range(M - 1):
        shared(wall, w_s, w_r, d).start()
        shared(prm, p_s, p_r, d).start()

    def plane_copy(j):
        return pltpu.make_async_remote_copy(
            src_ref=sendp.at[j], dst_ref=recvp.at[j], send_sem=pl_s.at[j], recv_sem=pl_r.at[j],
            device_id=(m, nxt), device_id_type=MESH)

    feat_copy.wait()
    for j in range(PZ):
        z = jnp.minimum(my_z + j, depth - 1)

        def stage(c, carry, z=z):
            staged[pl.ds(c * rows, rows), :] = featv[c, z].astype(f32)
            return carry

        lax.fori_loop(0, C, stage, 0, unroll=True)

        def pick(y, carry, j=j):
            sendp[j, y] = staged[pl.ds(my_y + y, C, stride=rows), :].astype(bf16)
            return carry

        lax.fori_loop(0, PY, pick, 0, unroll=True)
        plane_copy(j).start()

    inside = (v > 0).astype(f32)
    for j in range(PZ - 1):
        def stage(c, carry, j=j):
            own[pl.ds(j * C * rows + c * rows, rows), :] = featv[c, j].astype(f32) * inside
            return carry

        lax.fori_loop(0, C, stage, 0, unroll=True)

    int_copy.wait_recv()
    got = ints_in[...]
    prev_z = [jnp.sum(jnp.where(lane[0:1] == k, got[0:1], 0)) for k in range(MAXP)]
    prev_y = [jnp.sum(jnp.where(lane[0:1] == 4 + k, got[0:1], 0)) for k in range(MAXP)]
    prev_count = jnp.sum(jnp.where(lane[0:1] == 8, got[0:1], 0))
    at_z = chosen(lambda k: prev_z[k])
    at_y = chosen(lambda k: prev_y[k])

    first = m * PY
    own_off = [8 + jnp.clip(first - cy_ref[0, k], -8, 8) for k in range(MAXP)]
    in_off = [8 + jnp.clip(first - prev_y[k], -8, 8) for k in range(MAXP)]
    own_live = [(k < cnt_ref[0]).astype(f32) for k in range(MAXP)]
    in_live = [((k < prev_count) & (v > 0)).astype(f32) for k in range(MAXP)]

    def which(z):
        return 1 + jnp.clip(z, -1, PZ)

    def weigh(z, carry):
        total = jnp.zeros((PY, X), f32)
        for k in range(MAXP):
            total = total + gpad[which(z - cz_ref[0, k]), pl.ds(own_off[k], 8), :] * own_live[k]
            total = total + gpad[which(z + depth - prev_z[k]), pl.ds(in_off[k], 8), :] * in_live[k]
        inv[z] = 1.0 / jnp.maximum(total, 0.1)
        return carry

    lax.fori_loop(0, depth, weigh, 0, unroll=True)

    for d in range(M - 1):
        arrives(wall, w_s, w_r, d).wait_recv()
        arrives(prm, p_s, p_r, d).wait_recv()
    for q in range(M):
        r = q * C
        full = wall[q, :, 0:768]
        wa[r:r + C, 0:512] = full[:, 256:768]
        wa[128 + r:128 + r + C, :] = full
        wb[r:r + C, :] = full
        wb[128 + r:128 + r + C, 256:768] = full[:, 0:512]
        for o in range(PZ):
            for kz in range(3):
                j = o + kz - 1
                if 0 <= j < PZ:
                    w9[o * 128 + r:o * 128 + r + C, j * C:(j + 1) * C] = wall[q, :, 768 + kz * C:768 + (kz + 1) * C]

    def column(values):
        eye = lax.broadcasted_iota(jnp.int32, (C, C), 0) == lax.broadcasted_iota(jnp.int32, (C, C), 1)
        return jnp.sum(jnp.where(eye, jnp.broadcast_to(values, (C, C)), 0.0), axis=1, keepdims=True)

    gain = jnp.concatenate([column(prm[q, 0:1, 0:C]) for q in range(M)], axis=0)
    shift = jnp.concatenate([column(prm[q, 1:2, 0:C]) for q in range(M)], axis=0)
    for q in range(M):
        for o in range(2):
            at = o * 128 + q * C
            for k in range(K - 1):
                seg[k * 2 + o:k * 2 + o + 1, at:at + C] = prm[q, 2 + k:3 + k, 0:C]
                seg[8 + k * 2 + o:8 + k * 2 + o + 1, at:at + C] = prm[q, 4:5, 0:C]
    head = seg[...].astype(bf16)
    offsets = prm[0, 5:6, :] + prm[1, 5:6, :] + prm[2, 5:6, :] + prm[3, 5:6, :]
    offset = [jnp.sum(jnp.where(lane[0:1] == k, offsets, 0.0)) for k in range(K)]
    sub = lax.broadcasted_iota(jnp.int32, (8, 1), 0)
    bias = jnp.where(sub < 2, offset[0] - offset[2], offset[1] - offset[2])

    lane_row = lax.broadcasted_iota(jnp.int32, (C, X), 1)
    for j in range(PZ):
        plane_copy(j).wait_recv()
        beyond = at_z + j - depth
        start = jnp.clip(beyond, 0, PZ - 2) * (C * rows) + at_y

        def expand(y, carry, j=j, beyond=beyond, start=start):
            value = recvp[j, y].astype(f32)
            if j > 0:
                value = jnp.where(beyond >= 0, own[pl.ds(start + y, C, stride=rows), :], value)
            left = jnp.where(lane_row == 0, 0.0, pltpu.roll(value, 1, 1)).astype(bf16)
            right = jnp.where(lane_row == X - 1, 0.0, pltpu.roll(value, X - 1, 1)).astype(bf16)
            middle = value.astype(bf16)
            for ky in range(3):
                at = pl.ds(pl.multiple_of((y - ky + 2) * X, X), X)
                for kx, part in enumerate((left, middle, right)):
                    t = ky * 3 + kx
                    if t < 8:
                        im[j * 256 + t * C:j * 256 + (t + 1) * C, at] = part
                    else:
                        im9[j * C:(j + 1) * C, at] = part
            return carry

        lax.fori_loop(0, PY, expand, 0, unroll=True)

    sums[...] = jnp.zeros(sums.shape, f32)
    for p, taps in enumerate((wa, wb)):
        def conv(n, carry, p=p, taps=taps):
            at = pl.ds(pl.multiple_of(X + n * 256, X), 256)
            got = jnp.dot(taps[...], im[p * 256:p * 256 + 768, at], preferred_element_type=f32)
            got = got + jnp.dot(w9[p * 256:(p + 1) * 256, :], im9[:, at], preferred_element_type=f32)
            hid[p, :, pl.ds(pl.multiple_of(n * 256, 256), 256)] = got
            pair = got[:128] + got[128:]
            sums[...] += pair[:, :X] + pair[:, X:]
            return carry

        lax.fori_loop(0, 4, conv, 0, unroll=True)

    voxels = PZ * PY * X
    mean = jnp.sum(sums[...], axis=1, keepdims=True) / voxels
    sums[...] = jnp.zeros(sums.shape, f32)
    for p in range(2):
        def spread(n, carry, p=p):
            got = hid[p, :, pl.ds(pl.multiple_of(n * 256, 256), 256)]
            low = got[:128] - mean
            high = got[128:] - mean
            pair = low * low + high * high
            sums[...] += pair[:, :X] + pair[:, X:]
            return carry

        lax.fori_loop(0, 4, spread, 0, unroll=True)
    variance = jnp.sum(sums[...], axis=1, keepdims=True) / voxels
    scale = lax.rsqrt(variance + 1e-05) * gain

    alive = m < prev_count
    gx = bell_x((8, X))
    for p in range(2):
        gzp = jnp.where(sub % 2 == 0, f32(gz[2 * p]), f32(gz[2 * p + 1]))

        def classify(n, carry, p=p, gzp=gzp):
            parts = []
            for o in range(2):
                got = hid[p, o * 128:(o + 1) * 128, pl.ds(pl.multiple_of(n * 256, 256), 256)]
                normed = (got - mean) * scale + shift
                parts.append(jnp.maximum(normed, 0.01 * normed).astype(bf16))
            act = jnp.concatenate(parts, axis=0)
            both = jnp.dot(head, act, preferred_element_type=f32)
            logit = both[0:8] - both[8:16] + bias
            for h in range(2):
                y = n * 2 + h
                gyv = f32(gy[0])
                for i in range(1, PY):
                    gyv = jnp.where(y == i, f32(gy[i]), gyv)
                value = logit[:, h * X:(h + 1) * X] * (gx * gzp * gyv)
                value = jnp.where(alive, value, 0.0)
                tsend[p, pl.ds(y, 8, stride=8), :] = value
            return carry

        lax.fori_loop(0, 4, classify, 0, unroll=True)

    back = pltpu.make_async_remote_copy(
        src_ref=tsend.at[:, pl.ds(0, 32)], dst_ref=tback.at[m], send_sem=b_s, recv_sem=b_r,
        device_id=(m, prv), device_id_type=MESH)
    back.start()

    def across(d):
        return pltpu.make_async_remote_copy(
            src_ref=tsend.at[:, pl.ds(0, 32)], dst_ref=tin.at[m], send_sem=a_s.at[d], recv_sem=a_r.at[d],
            device_id=(mates[d], v), device_id_type=MESH)

    for d in range(M - 1):
        across(d).start()
    back.wait_recv()
    for d in range(M - 1):
        shared(tback, c_s, c_r, d).start()
    tin[m] = tsend[:, 0:32]

    def spread_out(buf, pad, s):
        for p in range(2):
            for k in range(K - 1):
                for o in range(2):
                    r = (k * 2 + o) * 8
                    pad[s, 1 + 2 * p + o, k, 8:16] = buf[s, p, r:r + 8]

    for d in range(M - 1):
        arrives(tin, a_s, a_r, d).wait_recv()
    for s in range(MAXP):
        spread_out(tin, pad_in, s)
    for d in range(M - 1):
        arrives(tback, c_s, c_r, d).wait_recv()
    for s in range(MAXP):
        spread_out(tback, pad_own, s)

    def finish(z, spill):
        diff = []
        for k in range(K - 1):
            total = jnp.zeros((PY, X), f32)
            for s in range(MAXP):
                total = total + pad_own[s, which(z - cz_ref[0, s]), k, pl.ds(own_off[s], 8), :]
                if spill:
                    total = total + pad_in[s, which(z + depth - prev_z[s]), k, pl.ds(in_off[s], 8), :] * inside
            diff.append(total * inv[z])
        top = jnp.maximum(jnp.maximum(diff[0], diff[1]), 0.0)
        powers = [jnp.exp(diff[0] - top), jnp.exp(diff[1] - top), jnp.exp(-top)]
        whole = 1.0 / (powers[0] + powers[1] + powers[2])
        for k in range(K):
            out_ref[k, z] = powers[k] * whole

    def rest(z, carry):
        finish(z, False)
        return carry

    for z in range(PZ - 1):
        finish(z, True)
    lax.fori_loop(PZ - 1, depth, rest, 0, unroll=True)

    int_copy.wait_send()
    for j in range(PZ):
        plane_copy(j).wait_send()
    back.wait_send()
    for d in range(M - 1):
        shared(wall, w_s, w_r, d).wait_send()
        shared(prm, p_s, p_r, d).wait_send()
        across(d).wait_send()
        shared(tback, c_s, c_r, d).wait_send()


def per_device(slabs, features, corner_z, corner_y, counts, conv_w, norm_gain, norm_shift, seg_w, seg_b):
    channels, depth, rows, width = features.shape
    taps = conv_w[0].transpose(2, 3, 4, 0, 1)
    dma = pltpu.SemaphoreType.DMA
    return pl.pallas_call(
        functools.partial(kernel, depth, slabs),
        name="ensemble_patches",
        out_shape=jax.ShapeDtypeStruct((K, depth, rows // M, width), f32),
        in_specs=[pl.BlockSpec(memory_space=pltpu.HBM)] * 9,
        out_specs=pl.BlockSpec(memory_space=pltpu.VMEM),
        scratch_shapes=[
            pltpu.SMEM((1, MAXP), jnp.int32),
            pltpu.SMEM((1, MAXP), jnp.int32),
            pltpu.SMEM((1,), jnp.int32),
            pltpu.VMEM((3, 3, 3, C, C), bf16),
            pltpu.VMEM((1, C), f32),
            pltpu.VMEM((1, C), f32),
            pltpu.VMEM((1, K, C), bf16),
            pltpu.VMEM((1, K), f32),
            pltpu.VMEM((channels, depth, rows, width), bf16),
            pltpu.VMEM((C * rows, X), f32),
            pltpu.VMEM(((PZ - 1) * C * rows, X), f32),
            pltpu.VMEM((8, X), jnp.int32),
            pltpu.VMEM((8, X), jnp.int32),
            pltpu.VMEM((PZ, PY, C, X), bf16),
            pltpu.VMEM((PZ, PY, C, X), bf16),
            pltpu.VMEM((M, C, 896), bf16),
            pltpu.VMEM((M, 8, X), f32),
            pltpu.VMEM((256, 768), bf16),
            pltpu.VMEM((256, 768), bf16),
            pltpu.VMEM((512, 128), bf16),
            pltpu.VMEM((16, 256), f32),
            pltpu.VMEM((PZ * 256, 10 * X), bf16),
            pltpu.VMEM((PZ * C, 10 * X), bf16),
            pltpu.VMEM((2, 256, PY * X), f32),
            pltpu.VMEM((128, X), f32),
            pltpu.VMEM((2, 64, X), f32),
            pltpu.VMEM((M, 2, 32, X), f32),
            pltpu.VMEM((M, 2, 32, X), f32),
            pltpu.VMEM((MAXP, PZ + 2, K - 1, 24, X), f32),
            pltpu.VMEM((MAXP, PZ + 2, K - 1, 24, X), f32),
            pltpu.VMEM((PZ + 2, 24, X), f32),
            pltpu.VMEM((depth, PY, X), f32),
            dma((8,)), dma, dma, dma, dma((PZ,)), dma((PZ,)), dma((3,)), dma((3,)), dma((3,)), dma((3,)),
            dma((3,)), dma((3,)), dma, dma, dma((3,)), dma((3,)),
        ],
        compiler_params=pltpu.CompilerParams(
            collective_id=0, has_side_effects=True, vmem_limit_bytes=40 * 1024 * 1024),
    )(*[
        arg if arg is counts else pltpu.with_memory_space_constraint(arg, pltpu.HBM)
        for arg in (features, corner_z, corner_y, counts, taps, norm_gain, norm_shift, seg_w, seg_b)])


def solution(mesh):
    placed = (
        P(None, "vol", None, None),
        P("vol", None),
        P("vol", None),
        P("vol"),
        P("member", None, None, None, None, None),
        P("member", None),
        P("member", None),
        P("member", None, None),
        P("member", None),
    )
    return jax.shard_map(
        functools.partial(per_device, mesh.shape["vol"]),
        mesh=mesh,
        in_specs=placed,
        out_specs=P(None, "vol", "member", None),
        check_vma=False,
    )
```
